256 devices in a mesh: dp: 4 (over x), seq: 64 (over y, z, core).
Axes of the slice: x: 4, y: 4, z: 8, core: 2. Of those that a mesh axis runs over, the one named last changes fastest.
Arguments:
- queries: bfloat16 [32768, 32, 128], P(('dp', 'seq')), parts along dimension 0, may hold values from -6 to 6
- keys: bfloat16 [32768, 4, 128], P(('dp', 'seq')), parts along dimension 0, may hold values from -6 to 6
- values: bfloat16 [32768, 4, 128], P(('dp', 'seq')), parts along dimension 0, may hold values from -6 to 6
- attn_out: bfloat16 [32768, 32, 128], P(('dp', 'seq')), parts along dimension 0, may hold values from -6 to 6
- out_grad: bfloat16 [32768, 32, 128], P(('dp', 'seq')), parts along dimension 0, may hold values from -1.5 to 1.5
- log_sums: float32 [32, 32768], P(None, ('dp', 'seq')), parts along dimension 1, may hold values from 2 to 4
- doc_ids: int32 [32768], P('dp'), parts along dimension 0, may hold values from 0 to 31, never falling along the last dimension, each value on 1 to 512 neighbouring positions
Outputs:
- query_grad: bfloat16 [32768, 32, 128], P(('dp', 'seq')), parts along dimension 0
- key_grad: bfloat16 [32768, 4, 128], P(('dp', 'seq')), parts along dimension 0
- value_grad: bfloat16 [32768, 4, 128], P(('dp', 'seq')), parts along dimension 0
The draws below stay inside these ranges and needn't reach their ends.
There are 4 independent parts, one for each index of `dp`. The reference program is written for one: setup_inputs(seed, part) draws one part's arguments, and reference() takes and returns one part's arrays. A program takes and returns all parts, laid end to end along the dimension named above; each array names one. Nothing has to cross between parts.
Inputs may be any that keep to these rules, and one draw needn't show every extreme that they name: `doc_ids`: document numbers never fall along the sequence; each document holds 1 to 512 positions, and one holds exactly 512.
All inputs are finite; a program needn't handle non-finite values.
Results may differ from the reference program's by a relative error of at most 0.009.
Values may be sent and summed in bfloat16 or wider, within the bound.
A program may use at most 64 MiB of HBM per device.

```python
import math
import jax
import jax.numpy as jnp
import numpy as np
from jax import lax

HEADS = 32
KV_HEADS = 4
HD = 128
TOK_DEV = 128
GROUP = 8
REACH = 4
DOC_MOST = 512
SEQ = 8192
DOCS = 32


def shard_levels(own_key, shape, split, least, top_value):
    gain = 1.0
    for dim, parts in split:
        steps = jax.random.uniform(jax.random.fold_in(jax.random.fold_in(own_key, 6), dim), (parts,), jnp.float32, least / len(split), top_value / len(split))
        gain = gain * jnp.repeat(jnp.exp(steps), shape[dim] // parts).reshape((-1,) + (1,) * (len(shape) - 1 - dim))
    return gain


def split_up(count, total, limit, slope):
    weights = [(1 << 20) // math.isqrt(grade ** slope) + 1 for grade in range(2, count + 1)]
    rest, counts = total - limit - (count - 1), [1] * (count - 1)
    while rest > 0:
        free = [i for i in range(count - 1) if counts[i] < limit]
        whole, budget = sum([weights[i] for i in free]), rest
        for i in free:
            more = min(limit - counts[i], max(1, budget * weights[i] // whole), rest)
            counts[i] = counts[i] + more
            rest = rest - more
    return np.array([limit] + counts)


def uneven(own_key, amount, total, limit, slope):
    if amount == 2:
        one = jax.random.randint(own_key, (), max(1, total - limit), min(limit, total - 1) + 1)
        return jnp.stack([one, total - one])
    sizes = jnp.asarray(split_up(amount, total, limit, slope), jnp.int32)
    twos = (amount - 1) // 2
    source_of, sink = sizes[1:1 + 2 * twos:2], sizes[2:2 + 2 * twos:2]
    room = jnp.minimum(source_of - 1, limit - sink)
    moved = jax.random.randint(jax.random.fold_in(own_key, 1), (twos,), 0, 1 << 20) % (room + 1)
    sizes = sizes.at[1:1 + 2 * twos:2].set(source_of - moved).at[2:2 + 2 * twos:2].set(sink + moved)
    return sizes[jax.random.permutation(jax.random.fold_in(own_key, 2), amount)]


def gaussian(stream_key, extent, scale, bound, pieces=(), kind=jnp.bfloat16):
    gain = shard_levels(stream_key, extent, pieces, -0.22, 0.18) if pieces else 1.0
    drawn = jax.random.normal(stream_key, extent, jnp.float32) * scale * gain
    return jnp.minimum(jnp.maximum(drawn, -bound), bound).astype(kind)


def setup_inputs(seed: int = 0, part: int = 0) -> dict:
    key_of = jax.random.split(jax.random.key(seed), 8)
    part_splits = jax.random.split(jax.random.fold_in(key_of[7], part), 8)
    queries = gaussian(part_splits[0], (SEQ, HEADS, HD), 1.0, 6.0, ((0, 64),))
    keys = gaussian(part_splits[1], (SEQ, KV_HEADS, HD), 1.0, 6.0, ((0, 64),))
    values = gaussian(part_splits[2], (SEQ, KV_HEADS, HD), 1.0, 6.0, ((0, 64),))
    attn_out = gaussian(part_splits[3], (SEQ, HEADS, HD), 1.0, 6.0, ((0, 64),))
    out_grad = gaussian(part_splits[4], (SEQ, HEADS, HD), 0.25, 1.5, ((0, 64),))
    log_sums = jnp.clip(2.0 + 2.0 * jax.random.uniform(part_splits[5], (HEADS, SEQ), jnp.float32) ** shard_levels(part_splits[5], (HEADS, SEQ), ((1, 64),), -0.2, 0.2), 2.0, 4.0)
    doc_ids = jnp.searchsorted(jnp.cumsum(uneven(part_splits[6], DOCS, SEQ, DOC_MOST, 1)), jnp.arange(SEQ), side="right").astype(jnp.int32)
    return dict(queries=queries, keys=keys, values=values, attn_out=attn_out, out_grad=out_grad, log_sums=log_sums, doc_ids=doc_ids)


def reference(queries, keys, values, attn_out, out_grad, log_sums, doc_ids):
    width = TOK_DEV
    span = (REACH + 1) * width
    margin = REACH * width
    scale = HD ** -0.5
    hi = lax.Precision.HIGHEST
    delta = jnp.sum(out_grad.astype(jnp.float32) * attn_out.astype(jnp.float32), axis=-1)
    key_pad = jnp.concatenate([jnp.zeros((margin, KV_HEADS, HD), keys.dtype), keys], 0)
    val_pad = jnp.concatenate([jnp.zeros((margin, KV_HEADS, HD), values.dtype), values], 0)
    doc_pad = jnp.concatenate([jnp.full((margin,), -1, jnp.int32), doc_ids.astype(jnp.int32)], 0)
    offsets = jnp.arange(width, dtype=jnp.int32)
    key_offsets = jnp.arange(span, dtype=jnp.int32)

    def block(carry, shard):
        key_acc, val_acc = carry
        start = (shard * width).astype(jnp.int32)
        query_blk = lax.dynamic_slice_in_dim(queries, start, width, 0).astype(jnp.float32).reshape(width, KV_HEADS, GROUP, HD)
        grad_blk = lax.dynamic_slice_in_dim(out_grad, start, width, 0).astype(jnp.float32).reshape(width, KV_HEADS, GROUP, HD)
        lse_blk = lax.dynamic_slice_in_dim(log_sums, start, width, 1).reshape(KV_HEADS, GROUP, width)
        delta_blk = lax.dynamic_slice_in_dim(delta, start, width, 0).T.reshape(KV_HEADS, GROUP, width)
        key_win = lax.dynamic_slice_in_dim(key_pad, start, span, 0).astype(jnp.float32)
        val_win = lax.dynamic_slice_in_dim(val_pad, start, span, 0).astype(jnp.float32)
        query_pos = start + offsets
        key_pos = start - margin + key_offsets
        query_doc = lax.dynamic_slice_in_dim(doc_ids.astype(jnp.int32), start, width, 0)
        key_doc = lax.dynamic_slice_in_dim(doc_pad, start, span, 0)
        live = (key_pos[None, :] <= query_pos[:, None]) & (key_doc[None, :] == query_doc[:, None]) & (key_pos[None, :] >= 0)
        scores = jnp.einsum("tkgd,skd->kgts", query_blk, key_win, precision=hi) * scale
        probs = jnp.where(live, jnp.exp(scores - lse_blk[..., None]), 0.0)
        dprobs = jnp.einsum("tkgd,skd->kgts", grad_blk, val_win, precision=hi)
        dscores = probs * (dprobs - delta_blk[..., None])
        probs_low = lax.optimization_barrier(probs.astype(jnp.bfloat16)).astype(jnp.float32)
        dscores_low = lax.optimization_barrier(dscores.astype(jnp.bfloat16)).astype(jnp.float32)
        query_part = jnp.einsum("kgts,skd->tkgd", dscores_low, key_win, precision=hi) * scale
        key_part = jnp.einsum("kgts,tkgd->skd", dscores_low, query_blk, precision=hi) * scale
        val_part = jnp.einsum("kgts,tkgd->skd", probs_low, grad_blk, precision=hi)
        key_part = lax.optimization_barrier(key_part.astype(jnp.bfloat16)).astype(jnp.float32)
        val_part = lax.optimization_barrier(val_part.astype(jnp.bfloat16)).astype(jnp.float32)
        key_acc = lax.dynamic_update_slice_in_dim(key_acc, lax.dynamic_slice_in_dim(key_acc, start, span, 0) + key_part, start, 0)
        val_acc = lax.dynamic_update_slice_in_dim(val_acc, lax.dynamic_slice_in_dim(val_acc, start, span, 0) + val_part, start, 0)
        return (key_acc, val_acc), query_part.reshape(width, HEADS, HD).astype(jnp.bfloat16)

    start_acc = jnp.zeros((margin + SEQ, KV_HEADS, HD), jnp.float32)
    (key_acc, val_acc), query_grad = lax.scan(block, (start_acc, start_acc), jnp.arange(SEQ // TOK_DEV, dtype=jnp.int32))
    query_grad = query_grad.reshape(SEQ, HEADS, HD)
    return query_grad, key_acc[margin:].astype(jnp.bfloat16), val_acc[margin:].astype(jnp.bfloat16)
```

```python
import functools

import jax
import jax.numpy as jnp
from jax import lax
from jax.experimental import pallas as pl
from jax.experimental.pallas import tpu as pltpu
from jax.sharding import PartitionSpec as P

F32 = jnp.float32
BF16 = jnp.bfloat16
MESH = pl.DeviceIdType.MESH
NT = (((1,), (1,)), ((), ()))
NN = (((1,), (0,)), ((), ()))
TN = (((0,), (0,)), ((), ()))
LOG2E = 1.4426950408889634


def dot(a, b, dims):
    return lax.dot_general(a, b, dims, preferred_element_type=F32)


def kernel(n_chips, width, group, scale,
           q_hbm, k_hbm, v_hbm, o_hbm, g_hbm, lse_hbm, doc_hbm,
           dq_out, dk_out, dv_out,
           qs, gs, os_, lse_in, docs, kin, vin, own_kv, kvb, bias, lse_b, dl_b, dq_acc, dq_send,
           parts, d0, ret, rb0, rb1, rb2,
           loc_sem, xs, xr, ks, kr0, kr1, fs, fr, rs0, rs1, rs2, rr0, rr1, rr2, dqs, dqr):
    me = lax.axis_index("seq")
    core = lax.rem(me, 2)
    chip = me // 2
    other = 1 - core
    rows = width * group

    def device(step, which):
        return {"seq": lax.rem(chip + step + n_chips, n_chips) * 2 + which}

    sibling = device(0, other)

    barrier = pltpu.get_barrier_semaphore()
    pl.semaphore_signal(barrier, inc=1, device_id=sibling, device_id_type=MESH)
    pl.semaphore_signal(barrier, inc=1, device_id=device(-1, 0), device_id_type=MESH)
    pl.semaphore_signal(barrier, inc=1, device_id=device(-1, 1), device_id_type=MESH)

    def remote(src, dst, send, recv, to):
        return pltpu.make_async_remote_copy(
            src_ref=src, dst_ref=dst, send_sem=send, recv_sem=recv, device_id=to, device_id_type=MESH
        )

    local = [
        pltpu.make_async_copy(k_hbm, kin, loc_sem.at[0]),
        pltpu.make_async_copy(v_hbm, vin, loc_sem.at[1]),
        pltpu.make_async_copy(doc_hbm, docs, loc_sem.at[2]),
        pltpu.make_async_copy(lse_hbm.at[pl.ds(2 * core, 2)], lse_in.at[:, core], loc_sem.at[3]),
    ]
    for j in range(2):
        for i, (src, dst) in enumerate(((q_hbm, qs), (g_hbm, gs), (o_hbm, os_))):
            local.append(
                pltpu.make_async_copy(src.at[:, 2 * core + j], dst.at[j, core], loc_sem.at[4 + 3 * j + i])
            )
    for copy in local:
        copy.start()

    local[0].wait()
    local[1].wait()
    own_kv[:, 0] = jnp.transpose(kin[...], (1, 0, 2))
    own_kv[:, 1] = jnp.transpose(vin[...], (1, 0, 2))
    for j in range(2):
        kvb[0, j, core] = own_kv[2 * core + j]

    local[2].wait()

    def mask_step(index, carry):
        back = index // 4
        key_half = lax.rem(index // 2, 2)
        query_half = lax.rem(index, 2)
        key_chip = chip - back
        key_row = lax.rem(key_chip + n_chips, n_chips) * 2 + key_half
        query_row = chip * 2 + query_half
        key_doc = docs[pl.ds(key_row, 1), :].astype(F32)
        query_doc = docs[pl.ds(query_row, 1), :].astype(F32)
        query_col = jnp.broadcast_to(query_doc, (width, width)).T
        t = lax.broadcasted_iota(jnp.int32, (width, width), 0) + query_row * width
        p = lax.broadcasted_iota(jnp.int32, (width, width), 1) + (key_chip * 2 + key_half) * width
        live = (query_col == key_doc) & (p <= t) & (p >= 0)
        block = jnp.where(live, 0.0, -jnp.inf).astype(F32)
        wide = jnp.broadcast_to(block[:, None, :], (width, group, width)).reshape(rows, width)
        bias[back, key_half, pl.ds(pl.multiple_of(query_half * rows, rows), rows), :] = wide
        return carry

    lax.fori_loop(0, 12, mask_step, 0)

    def row_terms(j, half):
        start = pl.multiple_of(half * rows, rows)
        row = lse_in[j, half] * LOG2E
        lse_b[j, pl.ds(start, rows), :] = jnp.broadcast_to(row.T[:, :, None], (width, group, 128)).reshape(rows, 128)
        g = gs[j, half].reshape(rows, 128).astype(F32)
        o = os_[j, half].reshape(rows, 128).astype(F32)
        dl_b[j, pl.ds(start, rows), :] = jnp.broadcast_to(jnp.sum(g * o, axis=-1, keepdims=True), (rows, 128))

    def block(j, back, key_half, half, halves, first):
        start = pl.multiple_of(half * rows, rows)
        count = rows * halves
        r = pl.ds(start, count)
        if halves == 1:
            q = qs[j, half].reshape(count, 128)
            g = gs[j, half].reshape(count, 128)
        else:
            q = qs[j].reshape(count, 128)
            g = gs[j].reshape(count, 128)
        k = kvb[back, j, key_half, 0]
        v = kvb[back, j, key_half, 1]
        s = dot(q, k, NT)
        dp = dot(g, v, NT)
        p = jnp.exp2(s * (scale * LOG2E) - lse_b[j, r, :] + bias[back, key_half, r, :])
        ds = (p * (dp - dl_b[j, r, :])).astype(BF16)
        p = p.astype(BF16)
        term = dot(ds, k, NN)
        if first:
            dq_acc[j, r, :] = term
        else:
            dq_acc[j, r, :] += term
        return dot(q, ds, TN) * scale, dot(g, p, TN)

    for copy in local[3:]:
        copy.wait()

    def own_step(j, carry):
        row_terms(j, core)
        dk, dv = block(j, 0, core, core, 1, True)
        parts[0, j, 0] = dk
        parts[0, j, 1] = dv
        return carry

    lax.fori_loop(0, 2, own_step, 0)

    pl.semaphore_wait(barrier, 3)

    sends = []
    for j in range(2):
        for x, which in enumerate((core, other)):
            sends.append(
                remote(own_kv.at[2 * which + j], kvb.at[1, j, core], ks.at[2 * j + x], kr1.at[j, core], device(1, which))
            )
    for copy in sends:
        copy.start()
    swaps = [
        remote(lse_hbm.at[pl.ds(2 * other, 2)], lse_in.at[:, core], xs.at[6], xr.at[6], sibling),
    ]
    for j in range(2):
        for i, (src, dst) in enumerate(((g_hbm, gs), (o_hbm, os_), (q_hbm, qs))):
            swaps.append(remote(src.at[:, 2 * other + j], dst.at[j, core], xs.at[3 * j + i], xr.at[3 * j + i], sibling))
        swaps.append(remote(own_kv.at[2 * other + j], kvb.at[0, j, core], ks.at[4 + j], kr0.at[j], sibling))
    for copy in swaps:
        copy.start()

    def arrival(dst, sem):
        return remote(dst, dst, fs.at[0], sem, sibling)

    arrival(lse_in.at[:, other], xr.at[6]).wait_recv()

    def sibling_step(j, carry):
        for i, dst in enumerate((gs, os_, qs)):
            arrival(dst.at[j, other], xr.at[3 * j + i]).wait_recv()
        row_terms(j, other)
        arrival(kvb.at[0, j, other], kr0.at[j]).wait_recv()
        dk, dv = block(j, 0, other, other, 1, True)
        parts[1, j, 0] = dk
        parts[1, j, 1] = dv
        dk, dv = block(j, 0, 0, 1, 1, False)
        parts[core, j, 0] += dk
        parts[core, j, 1] += dv
        ret[j] = parts[1, j].astype(BF16)
        remote(ret.at[j], rb0.at[j], rs0.at[j], rr0.at[j], sibling).start()
        return carry

    lax.fori_loop(0, 2, sibling_step, 0)

    def near_step(n, carry):
        j = n // 2
        a = jnp.where(lax.rem(n, 2) == 0, core, other)
        arrival(kvb.at[1, j, a], kr1.at[j, a]).wait_recv()
        remote(kvb.at[1, j, a], kvb.at[2, j, a], fs.at[n], fr.at[j, a], device(1, core)).start()
        dk, dv = block(j, 1, a, 0, 2, False)
        ret[2 + n, 0] = dk.astype(BF16)
        ret[2 + n, 1] = dv.astype(BF16)
        remote(ret.at[2 + n], rb1.at[2 * core + j], rs1.at[n], rr1.at[2 * core + j], device(-1, a)).start()
        return carry

    lax.fori_loop(0, 4, near_step, 0)

    def far_step(n, carry):
        j = n // 2
        a = jnp.where(lax.rem(n, 2) == 0, core, other)
        arrival(kvb.at[2, j, a], fr.at[j, a]).wait_recv()
        dk, dv = block(j, 2, a, 0, 1, False)
        ret[6 + n, 0] = dk.astype(BF16)
        ret[6 + n, 1] = dv.astype(BF16)

        @pl.when(a == 1)
        def _():
            dk2, dv2 = block(j, 2, a, 1, 1, False)
            ret[6 + n, 0] = (dk + dk2).astype(BF16)
            ret[6 + n, 1] = (dv + dv2).astype(BF16)

        remote(ret.at[6 + n], rb2.at[2 * core + j], rs2.at[n], rr2.at[2 * core + j], device(-2, a)).start()

        @pl.when(lax.rem(n, 2) == 1)
        def _():
            mine = dq_acc[j, pl.ds(pl.multiple_of(core * rows, rows), rows), :] * scale
            theirs = dq_acc[j, pl.ds(pl.multiple_of(other * rows, rows), rows), :] * scale
            dq_send[j] = theirs.astype(BF16).reshape(width, group, 128)
            remote(dq_send.at[j], dq_out.at[:, 2 * core + j], dqs.at[j], dqr.at[j], sibling).start()
            dq_out[:, 2 * core + j] = mine.astype(BF16).reshape(width, group, 128)

        return carry

    lax.fori_loop(0, 4, far_step, 0)

    for j in range(2):
        arrival(rb0.at[j], rr0.at[j]).wait_recv()
        d0[2 * core + j] = parts[0, j]
        d0[2 * other + j] = rb0[j].astype(F32)
    for h in range(4):
        arrival(rb1.at[h], rr1.at[h]).wait_recv()
    for h in range(4):
        arrival(rb2.at[h], rr2.at[h]).wait_recv()
    for i, out in enumerate((dk_out, dv_out)):
        heads = [(d0[h, i] + rb1[h, i].astype(F32) + rb2[h, i].astype(F32)).T for h in range(4)]
        out[...] = jnp.transpose(jnp.stack(heads), (1, 0, 2)).astype(BF16)

    for j in range(2):
        remote(dq_send.at[j], dq_out.at[:, 2 * other + j], dqs.at[j], dqr.at[j], sibling).wait()
        remote(ret.at[j], rb0.at[j], rs0.at[j], rr0.at[j], sibling).wait_send()
    for copy in sends + swaps:
        copy.wait_send()
    for n in range(4):
        remote(kvb.at[1, 0, 0], kvb.at[2, 0, 0], fs.at[n], fr.at[0, 0], sibling).wait_send()
        remote(ret.at[2 + n], rb1.at[0], rs1.at[n], rr1.at[0], sibling).wait_send()
        remote(ret.at[6 + n], rb2.at[0], rs2.at[n], rr2.at[0], sibling).wait_send()


def on_device(n_chips, queries, keys, values, attn_out, out_grad, log_sums, doc_ids):
    width, heads, size = queries.shape
    kv = keys.shape[1]
    group = heads // kv
    rows = width * group
    split = (width, kv, group, size)
    any_spec = pl.BlockSpec(memory_space=pl.ANY)
    vmem_spec = pl.BlockSpec(memory_space=pltpu.VMEM)
    dma = pltpu.SemaphoreType.DMA
    dq, dk, dv = pl.pallas_call(
        functools.partial(kernel, n_chips, width, group, size ** -0.5),
        out_shape=(
            jax.ShapeDtypeStruct(split, BF16),
            jax.ShapeDtypeStruct(keys.shape, BF16),
            jax.ShapeDtypeStruct(keys.shape, BF16),
        ),
        in_specs=[any_spec] * 7,
        out_specs=(vmem_spec,) * 3,
        scratch_shapes=[
            pltpu.VMEM((2, 2, width, group, size), BF16),
            pltpu.VMEM((2, 2, width, group, size), BF16),
            pltpu.VMEM((2, 2, width, group, size), BF16),
            pltpu.VMEM((2, 2, group, width), F32),
            pltpu.VMEM((2 * n_chips, width), jnp.int32),
            pltpu.VMEM(keys.shape, BF16),
            pltpu.VMEM(keys.shape, BF16),
            pltpu.VMEM((kv, 2, width, size), BF16),
            pltpu.VMEM((3, 2, 2, 2, width, size), BF16),
            pltpu.VMEM((3, 2, 2 * rows, width), F32),
            pltpu.VMEM((2, 2 * rows, 128), F32),
            pltpu.VMEM((2, 2 * rows, 128), F32),
            pltpu.VMEM((2, 2 * rows, size), F32),
            pltpu.VMEM((2, width, group, size), BF16),
            pltpu.VMEM((2, 2, 2, size, width), F32),
            pltpu.VMEM((kv, 2, size, width), F32),
            pltpu.VMEM((10, 2, size, width), BF16),
            pltpu.VMEM((2, 2, size, width), BF16),
            pltpu.VMEM((kv, 2, size, width), BF16),
            pltpu.VMEM((kv, 2, size, width), BF16),
            dma((10,)), dma((7,)), dma((7,)), dma((6,)), dma((2,)), dma((2, 2)), dma((4,)), dma((2, 2)),
            dma((2,)), dma((4,)), dma((4,)), dma((2,)), dma((4,)), dma((4,)), dma((2,)), dma((2,)),
        ],
        compiler_params=pltpu.CompilerParams(
            collective_id=0, has_side_effects=True, vmem_limit_bytes=60 * 2**20
        ),
    )(
        queries.reshape(split), keys, values, attn_out.reshape(split), out_grad.reshape(split),
        log_sums.reshape(kv, group, width), doc_ids.reshape(2 * n_chips, width),
    )
    return dq.reshape(queries.shape), dk, dv


def solution(mesh):
    placed = (
        P(("dp", "seq"), None, None),
        P(("dp", "seq"), None, None),
        P(("dp", "seq"), None, None),
        P(("dp", "seq"), None, None),
        P(("dp", "seq"), None, None),
        P(None, ("dp", "seq")),
        P("dp"),
    )
    return jax.shard_map(
        functools.partial(on_device, mesh.shape["seq"] // 2),
        mesh=mesh,
        in_specs=placed,
        out_specs=(P(("dp", "seq"), None, None),) * 3,
        check_vma=False,
    )
```

```python
import functools

import jax
import jax.numpy as jnp
from jax import lax
from jax.experimental import pallas as pl
from jax.experimental.pallas import tpu as pltpu
from jax.sharding import PartitionSpec as P

F32 = jnp.float32
BF16 = jnp.bfloat16
MESH = pl.DeviceIdType.MESH
NT = (((1,), (1,)), ((), ()))
NN = (((1,), (0,)), ((), ()))
TN = (((0,), (0,)), ((), ()))
LOG2E = 1.4426950408889634


def dot(a, b, dims):
    return lax.dot_general(a, b, dims, preferred_element_type=F32)


def kernel(n_chips, width, group, scale,
           q_hbm, k_hbm, v_hbm, o_hbm, g_hbm, lse_hbm, doc_hbm,
           dq_out, dk_out, dv_out,
           qs, gs, os_, lse_in, docs, kin, vin, own_kv, kvb, bias, lse_b, dl_b, dq_acc, dq_send,
           parts, d0, ret, rb0, rb1, rb2,
           loc_sem, xs, xr, ks, kr0, kr1, fs, fr, rs0, rs1, rs2, rr0, rr1, rr2, dqs, dqr):
    me = lax.axis_index("seq")
    core = lax.rem(me, 2)
    chip = me // 2
    other = 1 - core
    rows = width * group

    def device(step, which):
        return {"seq": lax.rem(chip + step + n_chips, n_chips) * 2 + which}

    sibling = device(0, other)

    barrier = pltpu.get_barrier_semaphore()
    pl.semaphore_signal(barrier, inc=1, device_id=sibling, device_id_type=MESH)
    pl.semaphore_signal(barrier, inc=1, device_id=device(-1, 0), device_id_type=MESH)
    pl.semaphore_signal(barrier, inc=1, device_id=device(-1, 1), device_id_type=MESH)

    def remote(src, dst, send, recv, to):
        return pltpu.make_async_remote_copy(
            src_ref=src, dst_ref=dst, send_sem=send, recv_sem=recv, device_id=to, device_id_type=MESH
        )

    local = [
        pltpu.make_async_copy(k_hbm, kin, loc_sem.at[0]),
        pltpu.make_async_copy(v_hbm, vin, loc_sem.at[1]),
        pltpu.make_async_copy(doc_hbm, docs, loc_sem.at[2]),
        pltpu.make_async_copy(lse_hbm.at[pl.ds(2 * core, 2)], lse_in.at[:, core], loc_sem.at[3]),
    ]
    for j in range(2):
        for i, (src, dst) in enumerate(((q_hbm, qs), (g_hbm, gs), (o_hbm, os_))):
            local.append(
                pltpu.make_async_copy(src.at[:, 2 * core + j], dst.at[j, core], loc_sem.at[4 + 3 * j + i])
            )
    for copy in local:
        copy.start()

    local[0].wait()
    local[1].wait()
    own_kv[:, 0] = jnp.transpose(kin[...], (1, 0, 2))
    own_kv[:, 1] = jnp.transpose(vin[...], (1, 0, 2))
    for j in range(2):
        kvb[0, j, core] = own_kv[2 * core + j]

    pl.semaphore_wait(barrier, 3)

    sends = []
    for j in range(2):
        for x, which in enumerate((core, other)):
            sends.append(
                remote(own_kv.at[2 * which + j], kvb.at[1, j, core], ks.at[2 * j + x], kr1.at[j, core], device(1, which))
            )
    for copy in sends:
        copy.start()
    swaps = [
        remote(lse_hbm.at[pl.ds(2 * other, 2)], lse_in.at[:, core], xs.at[6], xr.at[6], sibling),
    ]
    for j in range(2):
        for i, (src, dst) in enumerate(((g_hbm, gs), (o_hbm, os_), (q_hbm, qs))):
            swaps.append(remote(src.at[:, 2 * other + j], dst.at[j, core], xs.at[3 * j + i], xr.at[3 * j + i], sibling))
        swaps.append(remote(own_kv.at[2 * other + j], kvb.at[0, j, core], ks.at[4 + j], kr0.at[j], sibling))
    for copy in swaps:
        copy.start()

    local[2].wait()

    def mask_step(index, carry):
        back = index // 4
        key_half = lax.rem(index // 2, 2)
        query_half = lax.rem(index, 2)
        key_chip = chip - back
        key_row = lax.rem(key_chip + n_chips, n_chips) * 2 + key_half
        query_row = chip * 2 + query_half
        key_doc = docs[pl.ds(key_row, 1), :].astype(F32)
        query_doc = docs[pl.ds(query_row, 1), :].astype(F32)
        query_col = jnp.broadcast_to(query_doc, (width, width)).T
        t = lax.broadcasted_iota(jnp.int32, (width, width), 0) + query_row * width
        p = lax.broadcasted_iota(jnp.int32, (width, width), 1) + (key_chip * 2 + key_half) * width
        live = (query_col == key_doc) & (p <= t) & (p >= 0)
        block = jnp.where(live, 0.0, -jnp.inf).astype(F32)
        wide = jnp.broadcast_to(block[:, None, :], (width, group, width)).reshape(rows, width)
        bias[back, key_half, pl.ds(pl.multiple_of(query_half * rows, rows), rows), :] = wide
        return carry

    lax.fori_loop(0, 12, mask_step, 0)

    def row_terms(j, half):
        start = pl.multiple_of(half * rows, rows)
        row = lse_in[j, half] * LOG2E
        lse_b[j, pl.ds(start, rows), :] = jnp.broadcast_to(row.T[:, :, None], (width, group, 128)).reshape(rows, 128)
        g = gs[j, half].reshape(rows, 128).astype(F32)
        o = os_[j, half].reshape(rows, 128).astype(F32)
        dl_b[j, pl.ds(start, rows), :] = jnp.broadcast_to(jnp.sum(g * o, axis=-1, keepdims=True), (rows, 128))

    def block(j, back, key_half, half, halves, first):
        start = pl.multiple_of(half * rows, rows)
        count = rows * halves
        r = pl.ds(start, count)
        if halves == 1:
            q = qs[j, half].reshape(count, 128)
            g = gs[j, half].reshape(count, 128)
        else:
            q = qs[j].reshape(count, 128)
            g = gs[j].reshape(count, 128)
        k = kvb[back, j, key_half, 0]
        v = kvb[back, j, key_half, 1]
        s = dot(q, k, NT)
        dp = dot(g, v, NT)
        p = jnp.exp2(s * (scale * LOG2E) - lse_b[j, r, :] + bias[back, key_half, r, :])
        ds = (p * (dp - dl_b[j, r, :])).astype(BF16)
        p = p.astype(BF16)
        term = dot(ds, k, NN)
        if first:
            dq_acc[j, r, :] = term
        else:
            dq_acc[j, r, :] += term
        return dot(q, ds, TN) * scale, dot(g, p, TN)

    for copy in local[3:]:
        copy.wait()

    def own_step(j, carry):
        row_terms(j, core)
        dk, dv = block(j, 0, core, core, 1, True)
        parts[0, j, 0] = dk
        parts[0, j, 1] = dv
        return carry

    lax.fori_loop(0, 2, own_step, 0)

    def arrival(dst, sem):
        return remote(dst, dst, fs.at[0], sem, sibling)

    arrival(lse_in.at[:, other], xr.at[6]).wait_recv()

    def sibling_step(j, carry):
        for i, dst in enumerate((gs, os_, qs)):
            arrival(dst.at[j, other], xr.at[3 * j + i]).wait_recv()
        row_terms(j, other)
        arrival(kvb.at[0, j, other], kr0.at[j]).wait_recv()
        dk, dv = block(j, 0, other, other, 1, True)
        parts[1, j, 0] = dk
        parts[1, j, 1] = dv
        dk, dv = block(j, 0, 0, 1, 1, False)
        parts[core, j, 0] += dk
        parts[core, j, 1] += dv
        ret[j] = parts[1, j].astype(BF16)
        remote(ret.at[j], rb0.at[j], rs0.at[j], rr0.at[j], sibling).start()
        return carry

    lax.fori_loop(0, 2, sibling_step, 0)

    def near_step(n, carry):
        j = n // 2
        a = jnp.where(lax.rem(n, 2) == 0, core, other)
        arrival(kvb.at[1, j, a], kr1.at[j, a]).wait_recv()
        remote(kvb.at[1, j, a], kvb.at[2, j, a], fs.at[n], fr.at[j, a], device(1, core)).start()
        dk, dv = block(j, 1, a, 0, 2, False)
        ret[2 + n, 0] = dk.astype(BF16)
        ret[2 + n, 1] = dv.astype(BF16)
        remote(ret.at[2 + n], rb1.at[2 * core + j], rs1.at[n], rr1.at[2 * core + j], device(-1, a)).start()
        return carry

    lax.fori_loop(0, 4, near_step, 0)

    def far_step(n, carry):
        j = n // 2
        a = jnp.where(lax.rem(n, 2) == 0, core, other)
        arrival(kvb.at[2, j, a], fr.at[j, a]).wait_recv()
        dk, dv = block(j, 2, a, 0, 1, False)
        ret[6 + n, 0] = dk.astype(BF16)
        ret[6 + n, 1] = dv.astype(BF16)

        @pl.when(a == 1)
        def _():
            dk2, dv2 = block(j, 2, a, 1, 1, False)
            ret[6 + n, 0] = (dk + dk2).astype(BF16)
            ret[6 + n, 1] = (dv + dv2).astype(BF16)

        remote(ret.at[6 + n], rb2.at[2 * core + j], rs2.at[n], rr2.at[2 * core + j], device(-2, a)).start()

        @pl.when(lax.rem(n, 2) == 1)
        def _():
            mine = dq_acc[j, pl.ds(pl.multiple_of(core * rows, rows), rows), :] * scale
            theirs = dq_acc[j, pl.ds(pl.multiple_of(other * rows, rows), rows), :] * scale
            dq_send[j] = theirs.astype(BF16).reshape(width, group, 128)
            remote(dq_send.at[j], dq_out.at[:, 2 * core + j], dqs.at[j], dqr.at[j], sibling).start()
            dq_out[:, 2 * core + j] = mine.astype(BF16).reshape(width, group, 128)

        return carry

    lax.fori_loop(0, 4, far_step, 0)

    for j in range(2):
        arrival(rb0.at[j], rr0.at[j]).wait_recv()
        d0[2 * core + j] = parts[0, j]
        d0[2 * other + j] = rb0[j].astype(F32)
    for h in range(4):
        arrival(rb1.at[h], rr1.at[h]).wait_recv()
    for h in range(4):
        arrival(rb2.at[h], rr2.at[h]).wait_recv()
    for i, out in enumerate((dk_out, dv_out)):
        heads = [(d0[h, i] + rb1[h, i].astype(F32) + rb2[h, i].astype(F32)).T for h in range(4)]
        out[...] = jnp.transpose(jnp.stack(heads), (1, 0, 2)).astype(BF16)

    for j in range(2):
        remote(dq_send.at[j], dq_out.at[:, 2 * other + j], dqs.at[j], dqr.at[j], sibling).wait()
        remote(ret.at[j], rb0.at[j], rs0.at[j], rr0.at[j], sibling).wait_send()
    for copy in sends + swaps:
        copy.wait_send()
    for n in range(4):
        remote(kvb.at[1, 0, 0], kvb.at[2, 0, 0], fs.at[n], fr.at[0, 0], sibling).wait_send()
        remote(ret.at[2 + n], rb1.at[0], rs1.at[n], rr1.at[0], sibling).wait_send()
        remote(ret.at[6 + n], rb2.at[0], rs2.at[n], rr2.at[0], sibling).wait_send()


def hand_over(*refs):
    sems = refs[6]
    copies = [pltpu.make_async_copy(refs[i], refs[3 + i], sems.at[i]) for i in range(3)]
    for copy in copies:
        copy.start()
    for copy in copies:
        copy.wait()


def on_device(n_chips, queries, keys, values, attn_out, out_grad, log_sums, doc_ids):
    width, heads, size = queries.shape
    kv = keys.shape[1]
    group = heads // kv
    rows = width * group
    split = (width, kv, group, size)
    any_spec = pl.BlockSpec(memory_space=pl.ANY)
    vmem_spec = pl.BlockSpec(memory_space=pltpu.VMEM)
    dma = pltpu.SemaphoreType.DMA
    dq, dk, dv = pl.pallas_call(
        functools.partial(kernel, n_chips, width, group, size ** -0.5),
        out_shape=(
            pltpu.VMEM(split, BF16),
            pltpu.VMEM(keys.shape, BF16),
            pltpu.VMEM(keys.shape, BF16),
        ),
        in_specs=[any_spec] * 7,
        out_specs=(vmem_spec,) * 3,
        scratch_shapes=[
            pltpu.VMEM((2, 2, width, group, size), BF16),
            pltpu.VMEM((2, 2, width, group, size), BF16),
            pltpu.VMEM((2, 2, width, group, size), BF16),
            pltpu.VMEM((2, 2, group, width), F32),
            pltpu.VMEM((2 * n_chips, width), jnp.int32),
            pltpu.VMEM(keys.shape, BF16),
            pltpu.VMEM(keys.shape, BF16),
            pltpu.VMEM((kv, 2, width, size), BF16),
            pltpu.VMEM((3, 2, 2, 2, width, size), BF16),
            pltpu.VMEM((3, 2, 2 * rows, width), F32),
            pltpu.VMEM((2, 2 * rows, 128), F32),
            pltpu.VMEM((2, 2 * rows, 128), F32),
            pltpu.VMEM((2, 2 * rows, size), F32),
            pltpu.VMEM((2, width, group, size), BF16),
            pltpu.VMEM((2, 2, 2, size, width), F32),
            pltpu.VMEM((kv, 2, size, width), F32),
            pltpu.VMEM((10, 2, size, width), BF16),
            pltpu.VMEM((2, 2, size, width), BF16),
            pltpu.VMEM((kv, 2, size, width), BF16),
            pltpu.VMEM((kv, 2, size, width), BF16),
            dma((10,)), dma((7,)), dma((7,)), dma((6,)), dma((2,)), dma((2, 2)), dma((4,)), dma((2, 2)),
            dma((2,)), dma((4,)), dma((4,)), dma((2,)), dma((4,)), dma((4,)), dma((2,)), dma((2,)),
        ],
        compiler_params=pltpu.CompilerParams(
            collective_id=0, has_side_effects=True, vmem_limit_bytes=56 * 2**20
        ),
    )(
        queries.reshape(split), keys, values, attn_out.reshape(split), out_grad.reshape(split),
        log_sums.reshape(kv, group, width), doc_ids.reshape(2 * n_chips, width),
    )
    dq, dk, dv = pl.pallas_call(
        hand_over,
        out_shape=tuple(jax.ShapeDtypeStruct(x.shape, x.dtype) for x in (dq, dk, dv)),
        in_specs=[vmem_spec] * 3,
        out_specs=(any_spec,) * 3,
        scratch_shapes=[dma((3,))],
        compiler_params=pltpu.CompilerParams(vmem_limit_bytes=2**20),
    )(dq, dk, dv)
    return dq.reshape(queries.shape), dk, dv


def solution(mesh):
    placed = (
        P(("dp", "seq"), None, None),
        P(("dp", "seq"), None, None),
        P(("dp", "seq"), None, None),
        P(("dp", "seq"), None, None),
        P(("dp", "seq"), None, None),
        P(None, ("dp", "seq")),
        P("dp"),
    )
    return jax.shard_map(
        functools.partial(on_device, mesh.shape["seq"] // 2),
        mesh=mesh,
        in_specs=placed,
        out_specs=(P(("dp", "seq"), None, None),) * 3,
        check_vma=False,
    )
```

```python
import functools

import jax
import jax.numpy as jnp
from jax import lax
from jax.experimental import pallas as pl
from jax.experimental.pallas import tpu as pltpu
from jax.sharding import PartitionSpec as P

F32 = jnp.float32
BF16 = jnp.bfloat16
MESH = pl.DeviceIdType.MESH
NT = (((1,), (1,)), ((), ()))
NN = (((1,), (0,)), ((), ()))
TN = (((0,), (0,)), ((), ()))
LOG2E = 1.4426950408889634


def dot(a, b, dims):
    return lax.dot_general(a, b, dims, preferred_element_type=F32)


def kernel(n_chips, width, group, scale,
           q_hbm, k_hbm, v_hbm, o_hbm, g_hbm, lse_hbm, doc_hbm,
           dq_out, dk_out, dv_out,
           qs, gs, os_, lse_in, docs, kin, vin, own_kv, kvb, bias, lse_b, dl_b, dq_acc, dq_send,
           parts, near, far, ret0, ret1, ret2, rb0, rb1, rb2, pre, total,
           loc_sem, xs, xr, ks, ks0, kr0, kr1, fs, fr, rs0, rs1, rs2, rr0, rr1, rr2, rp, dqs, dqr):
    me = lax.axis_index("seq")
    core = lax.rem(me, 2)
    chip = me // 2
    other = 1 - core
    rows = width * group

    def device(step, which):
        return {"seq": lax.rem(chip + step + n_chips, n_chips) * 2 + which}

    sibling = device(0, other)

    barrier = pltpu.get_barrier_semaphore()
    pl.semaphore_signal(barrier, inc=1, device_id=device(-1, 0), device_id_type=MESH)
    pl.semaphore_signal(barrier, inc=1, device_id=device(-1, 1), device_id_type=MESH)
    pl.semaphore_signal(barrier, inc=1, device_id=sibling, device_id_type=MESH)

    def remote(src, dst, send, recv, to):
        return pltpu.make_async_remote_copy(
            src_ref=src, dst_ref=dst, send_sem=send, recv_sem=recv, device_id=to, device_id_type=MESH
        )

    def arrived(dst, sem):
        remote(dst, dst, xs.at[0], sem, sibling).wait_recv()

    def sent(src, sem):
        remote(src, src, sem, xr.at[0], sibling).wait_send()

    local = [
        pltpu.make_async_copy(k_hbm, kin, loc_sem.at[0]),
        pltpu.make_async_copy(v_hbm, vin, loc_sem.at[1]),
        pltpu.make_async_copy(doc_hbm, docs, loc_sem.at[2]),
        pltpu.make_async_copy(lse_hbm.at[pl.ds(2 * core, 2)], lse_in.at[:, core], loc_sem.at[3]),
    ]
    for j in range(2):
        for i, (src, dst) in enumerate(((q_hbm, qs), (g_hbm, gs), (o_hbm, os_))):
            local.append(
                pltpu.make_async_copy(src.at[:, 2 * core + j], dst.at[j, core], loc_sem.at[4 + 3 * j + i])
            )
    for copy in local:
        copy.start()

    local[0].wait()
    own_kv[:, 0] = jnp.transpose(kin[...], (1, 0, 2))
    local[1].wait()
    own_kv[:, 1] = jnp.transpose(vin[...], (1, 0, 2))

    pl.semaphore_wait(barrier, 3)

    def half_of(n):
        return (core, other)[n % 2]

    def own(n):
        j, which = n // 2, half_of(n)
        return [
            remote(own_kv.at[2 * which + j, p], kvb.at[1, j, core, p], ks.at[n, p], kr1.at[j, core, p], device(1, which))
            for p in range(2)
        ]

    for n in range(3):
        for copy in own(n):
            copy.start()
    swaps = [remote(lse_hbm.at[pl.ds(2 * other, 2)], lse_in.at[:, core], xs.at[6], xr.at[6], sibling)]
    for j in range(2):
        for i, (src, dst) in enumerate(((g_hbm, gs), (o_hbm, os_), (q_hbm, qs))):
            swaps.append(remote(src.at[:, 2 * other + j], dst.at[j, core], xs.at[3 * j + i], xr.at[3 * j + i], sibling))
        swaps.append(remote(own_kv.at[2 * other + j], kvb.at[0, j, core], ks0.at[j], kr0.at[j], sibling))
    for copy in swaps:
        copy.start()

    for j in range(2):
        kvb[0, j, core] = own_kv[2 * core + j]

    local[2].wait()

    def mask_step(index, carry):
        back = index // 4
        key_half = lax.rem(index // 2, 2)
        query_half = lax.rem(index, 2)
        key_chip = chip - back
        key_row = lax.rem(key_chip + n_chips, n_chips) * 2 + key_half
        query_row = chip * 2 + query_half
        key_doc = docs[pl.ds(key_row, 1), :].astype(F32)
        query_doc = docs[pl.ds(query_row, 1), :].astype(F32)
        query_col = jnp.broadcast_to(query_doc, (width, width)).T
        t = lax.broadcasted_iota(jnp.int32, (width, width), 0) + query_row * width
        p = lax.broadcasted_iota(jnp.int32, (width, width), 1) + (key_chip * 2 + key_half) * width
        live = (query_col == key_doc) & (p <= t) & (p >= 0)
        block = jnp.where(live, 0.0, -jnp.inf).astype(F32)
        wide = jnp.broadcast_to(block[:, None, :], (width, group, width)).reshape(rows, width)
        bias[back, key_half, pl.ds(pl.multiple_of(query_half * rows, rows), rows), :] = wide
        return carry

    lax.fori_loop(0, 12, mask_step, 0)

    def row_terms(j, half):
        start = pl.multiple_of(half * rows, rows)
        row = lse_in[j, half] * LOG2E
        lse_b[j, pl.ds(start, rows), :] = jnp.broadcast_to(row.T[:, :, None], (width, group, 128)).reshape(rows, 128)
        g = gs[j, half].reshape(rows, 128).astype(F32)
        o = os_[j, half].reshape(rows, 128).astype(F32)
        dl_b[j, pl.ds(start, rows), :] = jnp.broadcast_to(jnp.sum(g * o, axis=-1, keepdims=True), (rows, 128))

    def block(j, back, key_half, half, first=False):
        r = pl.ds(pl.multiple_of(half * rows, rows), rows)
        q = qs[j, half].reshape(rows, 128)
        g = gs[j, half].reshape(rows, 128)
        k = kvb[back, j, key_half, 0]
        v = kvb[back, j, key_half, 1]
        s = dot(q, k, NT)
        dp = dot(g, v, NT)
        p = jnp.exp2(s * (scale * LOG2E) - lse_b[j, r, :] + bias[back, key_half, r, :])
        ds = (p * (dp - dl_b[j, r, :])).astype(BF16)
        p = p.astype(BF16)
        term = dot(ds, k, NN)
        if first:
            dq_acc[j, r, :] = term
        else:
            dq_acc[j, r, :] += term
        return dot(q, ds, TN) * scale, dot(g, p, TN)

    for copy in local[3:]:
        copy.wait()

    def own_step(j, carry):
        row_terms(j, core)
        dk, dv = block(j, 0, core, core, True)
        parts[0, j, 0] = dk
        parts[0, j, 1] = dv
        return carry

    lax.fori_loop(0, 2, own_step, 0)

    arrived(lse_in.at[:, other], xr.at[6])

    def swap_terms(j):
        for i, dst in enumerate((gs, os_)):
            arrived(dst.at[j, other], xr.at[3 * j + i])
        row_terms(j, other)

    def sibling_keys(j, first):
        arrived(qs.at[j, other], xr.at[3 * j + 2])
        arrived(kvb.at[0, j, other], kr0.at[j])
        dk, dv = block(j, 0, other, other, first)
        parts[1, j, 0] = dk
        parts[1, j, 1] = dv

    def late_rows(j):
        dk, dv = block(j, 0, 0, 1)
        parts[core, j, 0] += dk
        parts[core, j, 1] += dv
        ret0[j] = parts[1, j].astype(BF16)
        remote(ret0.at[j], rb0.at[j], rs0.at[j], rr0.at[j], sibling).start()

    def forward(n, p):
        j, a = n // 2, half_of(n)
        arrived(kvb.at[1, j, a, p], kr1.at[j, a, p])
        remote(kvb.at[1, j, a, p], kvb.at[2, j, a, p], fs.at[n, p], fr.at[j, a, p], device(1, core)).start()

    def give_near(n, p):
        j, a = n // 2, half_of(n)
        remote(ret1.at[n, p], rb1.at[2 * core + j, p], rs1.at[n, p], rr1.at[2 * core + j, p], device(-1, a)).start()

    def near_own(n):
        dk, dv = block(n // 2, 1, half_of(n), core)
        near[n, 0] = dk
        near[n, 1] = dv

    def near_other(n, first=False):
        dk, dv = block(n // 2, 1, half_of(n), other, first)
        near[n, 0] += dk
        near[n, 1] += dv

    def far_block(n):
        j, a = n // 2, half_of(n)
        for p in range(2):
            arrived(kvb.at[2, j, a, p], fr.at[j, a, p])
        dk, dv = block(j, 2, a, 0)
        far[0] = dk
        far[1] = dv

        @pl.when(a == 1)
        def _():
            dk2, dv2 = block(j, 2, a, 1)
            far[0] += dk2
            far[1] += dv2

        for p in range(2):
            ret2[n, p] = far[p].astype(BF16)
            if n == 0:
                remote(ret2.at[0, p], rb2.at[p], rs2.at[0, p], rr2.at[p], device(-2, a)).start()
            else:
                remote(ret2.at[n, p], pre.at[n, p], rs2.at[n, p], rp.at[n, p], device(-1, core)).start()

    def pass_on(n, p):
        arrived(pre.at[n, p], rp.at[n, p])
        ret1[n, p] = (near[n, p] + pre[n, p].astype(F32)).astype(BF16)
        give_near(n, p)

    def give_queries(j):
        theirs = dq_acc[j, pl.ds(pl.multiple_of(other * rows, rows), rows), :] * scale
        dq_send[j] = theirs.astype(BF16).reshape(width, group, 128)
        remote(dq_send.at[j], dq_out.at[:, 2 * core + j], dqs.at[j], dqr.at[j], sibling).start()
        mine = dq_acc[j, pl.ds(pl.multiple_of(core * rows, rows), rows), :] * scale
        dq_out[:, 2 * core + j] = mine.astype(BF16).reshape(width, group, 128)

    swap_terms(0)
    sibling_keys(0, True)
    forward(0, 0)
    late_rows(0)
    forward(0, 1)
    for copy in own(3):
        copy.start()
    near_own(0)
    forward(1, 0)
    near_other(0)
    for p in range(2):
        ret1[0, p] = near[0, p].astype(BF16)
        give_near(0, p)
    forward(1, 1)
    near_own(1)
    near_other(1)
    forward(2, 0)
    swap_terms(1)
    forward(2, 1)
    sibling_keys(1, True)
    near_own(2)
    near_other(2)
    far_block(0)
    forward(3, 0)
    late_rows(1)
    forward(3, 1)
    near_own(3)
    near_other(3)
    far_block(1)
    give_queries(0)
    far_block(2)
    far_block(3)
    give_queries(1)
    for n in range(1, 4):
        for p in range(2):
            pass_on(n, p)

    for n in range(4):
        j = n // 2
        h = 2 * half_of(n) + j
        if n % 2 == 1:
            arrived(rb0.at[j], rr0.at[j])
        for p in range(2):
            arrived(rb1.at[h, p], rr1.at[h, p])
            acc = rb1[h, p].astype(F32) + (parts[0, j, p] if n % 2 == 0 else rb0[j, p].astype(F32))
            if n == 0:
                arrived(rb2.at[p], rr2.at[p])
                acc = acc + rb2[p].astype(F32)
            total[p, h] = acc.T
    dk_out[...] = jnp.transpose(total[0], (1, 0, 2)).astype(BF16)
    dv_out[...] = jnp.transpose(total[1], (1, 0, 2)).astype(BF16)

    for j in range(2):
        arrived(dq_out.at[:, 2 * other + j], dqr.at[j])
        sent(dq_send.at[j], dqs.at[j])
        sent(ret0.at[j], rs0.at[j])
    for copy in swaps:
        copy.wait_send()
    for n in range(4):
        for p in range(2):
            sent(own_kv.at[0, p], ks.at[n, p])
            sent(kvb.at[1, 0, 0, p], fs.at[n, p])
            sent(ret1.at[n, p], rs1.at[n, p])
            sent(ret2.at[n, p], rs2.at[n, p])


def hand_over(*refs):
    sems = refs[6]
    copies = [pltpu.make_async_copy(refs[i], refs[3 + i], sems.at[i]) for i in range(3)]
    for copy in copies:
        copy.start()
    for copy in copies:
        copy.wait()


def on_device(n_chips, queries, keys, values, attn_out, out_grad, log_sums, doc_ids):
    width, heads, size = queries.shape
    kv = keys.shape[1]
    group = heads // kv
    rows = width * group
    split = (width, kv, group, size)
    any_spec = pl.BlockSpec(memory_space=pl.ANY)
    vmem_spec = pl.BlockSpec(memory_space=pltpu.VMEM)
    dma = pltpu.SemaphoreType.DMA
    dq, dk, dv = pl.pallas_call(
        functools.partial(kernel, n_chips, width, group, size ** -0.5),
        out_shape=(
            pltpu.VMEM(split, BF16),
            pltpu.VMEM(keys.shape, BF16),
            pltpu.VMEM(keys.shape, BF16),
        ),
        in_specs=[any_spec] * 7,
        out_specs=(vmem_spec,) * 3,
        scratch_shapes=[
            pltpu.VMEM((2, 2, width, group, size), BF16),
            pltpu.VMEM((2, 2, width, group, size), BF16),
            pltpu.VMEM((2, 2, width, group, size), BF16),
            pltpu.VMEM((2, 2, group, width), F32),
            pltpu.VMEM((2 * n_chips, width), jnp.int32),
            pltpu.VMEM(keys.shape, BF16),
            pltpu.VMEM(keys.shape, BF16),
            pltpu.VMEM((kv, 2, width, size), BF16),
            pltpu.VMEM((3, 2, 2, 2, width, size), BF16),
            pltpu.VMEM((3, 2, 2 * rows, width), F32),
            pltpu.VMEM((2, 2 * rows, 128), F32),
            pltpu.VMEM((2, 2 * rows, 128), F32),
            pltpu.VMEM((2, 2 * rows, size), F32),
            pltpu.VMEM((2, width, group, size), BF16),
            pltpu.VMEM((2, 2, 2, size, width), F32),
            pltpu.VMEM((4, 2, size, width), F32),
            pltpu.VMEM((2, size, width), F32),
            pltpu.VMEM((2, 2, size, width), BF16),
            pltpu.VMEM((4, 2, size, width), BF16),
            pltpu.VMEM((4, 2, size, width), BF16),
            pltpu.VMEM((2, 2, size, width), BF16),
            pltpu.VMEM((kv, 2, size, width), BF16),
            pltpu.VMEM((2, size, width), BF16),
            pltpu.VMEM((4, 2, size, width), BF16),
            pltpu.VMEM((2, kv, width, size), F32),
            dma((10,)), dma((7,)), dma((7,)), dma((4, 2)), dma((2,)), dma((2,)), dma((2, 2, 2)), dma((4, 2)),
            dma((2, 2, 2)), dma((2,)), dma((4, 2)), dma((4, 2)), dma((2,)), dma((kv, 2)), dma((2,)), dma((4, 2)),
            dma((2,)), dma((2,)),
        ],
        compiler_params=pltpu.CompilerParams(
            collective_id=0, has_side_effects=True, vmem_limit_bytes=56 * 2**20
        ),
    )(
        queries.reshape(split), keys, values, attn_out.reshape(split), out_grad.reshape(split),
        log_sums.reshape(kv, group, width), doc_ids.reshape(2 * n_chips, width),
    )
    dq, dk, dv = pl.pallas_call(
        hand_over,
        out_shape=tuple(jax.ShapeDtypeStruct(x.shape, x.dtype) for x in (dq, dk, dv)),
        in_specs=[vmem_spec] * 3,
        out_specs=(any_spec,) * 3,
        scratch_shapes=[dma((3,))],
        compiler_params=pltpu.CompilerParams(vmem_limit_bytes=2**20),
    )(dq, dk, dv)
    return dq.reshape(queries.shape), dk, dv


def solution(mesh):
    placed = (
        P(("dp", "seq"), None, None),
        P(("dp", "seq"), None, None),
        P(("dp", "seq"), None, None),
        P(("dp", "seq"), None, None),
        P(("dp", "seq"), None, None),
        P(None, ("dp", "seq")),
        P("dp"),
    )
    return jax.shard_map(
        functools.partial(on_device, mesh.shape["seq"] // 2),
        mesh=mesh,
        in_specs=placed,
        out_specs=(P(("dp", "seq"), None, None),) * 3,
        check_vma=False,
    )
```

```python
import functools

import jax
import jax.numpy as jnp
from jax import lax
from jax.experimental import pallas as pl
from jax.experimental.pallas import tpu as pltpu
from jax.sharding import PartitionSpec as P

F32 = jnp.float32
BF16 = jnp.bfloat16
MESH = pl.DeviceIdType.MESH
NT = (((1,), (1,)), ((), ()))
NN = (((1,), (0,)), ((), ()))
TN = (((0,), (0,)), ((), ()))
LOG2E = 1.4426950408889634


def dot(a, b, dims):
    return lax.dot_general(a, b, dims, preferred_element_type=F32)


def kernel(n_chips, width, group, scale,
           q_hbm, k_hbm, v_hbm, o_hbm, g_hbm, lse_hbm, doc_hbm,
           dq_out, dk_out, dv_out,
           qs, gs, os_, lse_in, docs, kin, vin, own_kv, kvb, bias0, bias1, bias2, lse_b0, lse_b1, dl_b0, dl_b1, dq_acc0, dq_acc1, dq_send,
           parts, near, far, ret0, ret1, ret2, rb0, rb1, rb2, pre, total,
           loc_sem, xs, xr, ks, ks0, kr0, kr1, fs, fr, rs0, rs1, rs2, rr0, rr1, rr2, rp, dqs, dqr):
    lse_b, dl_b, dq_acc = (lse_b0, lse_b1), (dl_b0, dl_b1), (dq_acc0, dq_acc1)
    bias = (bias0, bias1, bias2)
    me = lax.axis_index("seq")
    core = lax.rem(me, 2)
    chip = me // 2
    other = 1 - core
    rows = width * group

    def device(step, which):
        return {"seq": lax.rem(chip + step + n_chips, n_chips) * 2 + which}

    sibling = device(0, other)
    has_prev, has_next = chip > 0, chip < n_chips - 1
    has_prev2, has_next2 = chip > 1, chip < n_chips - 2

    barrier = pltpu.get_barrier_semaphore()

    @pl.when(has_prev)
    def _():
        pl.semaphore_signal(barrier, inc=1, device_id=device(-1, 0), device_id_type=MESH)
        pl.semaphore_signal(barrier, inc=1, device_id=device(-1, 1), device_id_type=MESH)

    pl.semaphore_signal(barrier, inc=1, device_id=sibling, device_id_type=MESH)

    def remote(src, dst, send, recv, to):
        return pltpu.make_async_remote_copy(
            src_ref=src, dst_ref=dst, send_sem=send, recv_sem=recv, device_id=to, device_id_type=MESH
        )

    def arrived(dst, sem, there=None):
        def wait():
            remote(dst, dst, xs.at[0], sem, sibling).wait_recv()

        wait() if there is None else pl.when(there)(wait)

    def sent(src, sem, there=None):
        def wait():
            remote(src, src, sem, xr.at[0], sibling).wait_send()

        wait() if there is None else pl.when(there)(wait)

    def start(copies, there):
        @pl.when(there)
        def _():
            for copy in copies:
                copy.start()

    @pl.when(chip == 0)
    def _():
        kvb[1] = jnp.zeros_like(kvb[1])

    @pl.when(jnp.logical_not(has_prev2))
    def _():
        kvb[2] = jnp.zeros_like(kvb[2])

    @pl.when(jnp.logical_not(has_next))
    def _():
        rb1[...] = jnp.zeros_like(rb1)

    @pl.when(jnp.logical_not(has_next & has_prev))
    def _():
        pre[...] = jnp.zeros_like(pre)

    @pl.when(jnp.logical_not(has_next2))
    def _():
        rb2[...] = jnp.zeros_like(rb2)

    local = [
        pltpu.make_async_copy(k_hbm, kin, loc_sem.at[0]),
        pltpu.make_async_copy(v_hbm, vin, loc_sem.at[1]),
        pltpu.make_async_copy(doc_hbm, docs, loc_sem.at[2]),
        pltpu.make_async_copy(lse_hbm.at[pl.ds(2 * core, 2)], lse_in.at[:, core], loc_sem.at[3]),
    ]
    for j in range(2):
        for i, (src, dst) in enumerate(((q_hbm, qs), (g_hbm, gs), (o_hbm, os_))):
            local.append(
                pltpu.make_async_copy(src.at[:, 2 * core + j], dst.at[j, core], loc_sem.at[4 + 3 * j + i])
            )
    for copy in local:
        copy.start()

    local[0].wait()
    own_kv[:, 0] = jnp.transpose(kin[...], (1, 0, 2))
    local[1].wait()
    own_kv[:, 1] = jnp.transpose(vin[...], (1, 0, 2))

    pl.semaphore_wait(barrier, jnp.where(has_next, 3, 1))

    def half_of(n):
        return (core, other)[n % 2]

    def own(n):
        j, which = n // 2, half_of(n)
        return [
            remote(own_kv.at[2 * which + j, p], kvb.at[1, j, core, p], ks.at[n, p], kr1.at[j, core, p], device(1, which))
            for p in range(2)
        ]

    start(own(0) + own(1) + own(2), has_next)
    swaps = [remote(lse_hbm.at[pl.ds(2 * other, 2)], lse_in.at[:, core], xs.at[6], xr.at[6], sibling)]
    for j in range(2):
        for i, (src, dst) in enumerate(((g_hbm, gs), (o_hbm, os_), (q_hbm, qs))):
            swaps.append(remote(src.at[:, 2 * other + j], dst.at[j, core], xs.at[3 * j + i], xr.at[3 * j + i], sibling))
        swaps.append(remote(own_kv.at[2 * other + j], kvb.at[0, j, core], ks0.at[j], kr0.at[j], sibling))
    for copy in swaps:
        copy.start()

    for j in range(2):
        kvb[0, j, core] = own_kv[2 * core + j]

    local[2].wait()

    def mask(back, query_half, key_half):
        key_chip = chip - back
        key_row = lax.rem(key_chip + n_chips, n_chips) * 2 + key_half
        query_row = chip * 2 + query_half
        key_doc = docs[pl.ds(key_row, 1), :].astype(F32)
        query_doc = docs[pl.ds(query_row, 1), :].astype(F32)
        query_col = jnp.broadcast_to(query_doc, (width, width)).T
        t = lax.broadcasted_iota(jnp.int32, (width, width), 0) + query_row * width
        p = lax.broadcasted_iota(jnp.int32, (width, width), 1) + (key_chip * 2 + key_half) * width
        live = (query_col == key_doc) & (p <= t) & (p >= 0)
        value = jnp.where(live, 0.0, -jnp.inf).astype(F32)
        wide = jnp.broadcast_to(value[:, None, :], (width, group, width)).reshape(rows, width)
        bias[back][key_half, query_half * rows:(query_half + 1) * rows, :] = wide

    for query_half, key_half in ((0, 0), (1, 0), (1, 1)):
        mask(0, query_half, key_half)

    def row_terms(j, half):
        start = pl.multiple_of(half * rows, rows)
        row = lse_in[j, half] * LOG2E
        lse_b[j][pl.ds(start, rows), :] = jnp.broadcast_to(row.T[:, :, None], (width, group, 128)).reshape(rows, 128)
        g = gs[j, half].reshape(rows, 128).astype(F32)
        o = os_[j, half].reshape(rows, 128).astype(F32)
        dl_b[j][pl.ds(start, rows), :] = jnp.broadcast_to(jnp.sum(g * o, axis=-1, keepdims=True), (rows, 128))

    def block(j, back, key_half, half, first=False):
        r = pl.ds(pl.multiple_of(half * rows, rows), rows)
        q = qs[j, half].reshape(rows, 128)
        g = gs[j, half].reshape(rows, 128)
        k = kvb[back, j, key_half, 0]
        v = kvb[back, j, key_half, 1]
        s = dot(q, k, NT)
        dp = dot(g, v, NT)
        p = jnp.exp2(s * (scale * LOG2E) - lse_b[j][r, :] + bias[back][key_half, r, :])
        ds = (p * (dp - dl_b[j][r, :])).astype(BF16)
        p = p.astype(BF16)
        term = dot(ds, k, NN)
        if first:
            dq_acc[j][r, :] = term
        else:
            dq_acc[j][r, :] += term
        return dot(q, ds, TN) * scale, dot(g, p, TN)

    for copy in local[3:]:
        copy.wait()

    for j in range(2):
        row_terms(j, core)
    for j in range(2):
        mask(1, j, 0)
        mask(1, j, 1)
        dk, dv = block(j, 0, core, core, True)
        parts[0, j, 0] = dk
        parts[0, j, 1] = dv

    arrived(lse_in.at[:, other], xr.at[6])

    def swap_wait(j):
        for i, dst in enumerate((gs, os_)):
            arrived(dst.at[j, other], xr.at[3 * j + i])

    def sibling_keys(j, first):
        arrived(qs.at[j, other], xr.at[3 * j + 2])
        arrived(kvb.at[0, j, other], kr0.at[j])
        dk, dv = block(j, 0, other, other, first)
        parts[1, j, 0] = dk
        parts[1, j, 1] = dv

    def late_rows(j):
        dk, dv = block(j, 0, 0, 1)
        parts[core, j, 0] += dk
        parts[core, j, 1] += dv
        ret0[j] = parts[1, j].astype(BF16)
        remote(ret0.at[j], rb0.at[j], rs0.at[j], rr0.at[j], sibling).start()

    def forward(n, p):
        j, a = n // 2, half_of(n)
        arrived(kvb.at[1, j, a, p], kr1.at[j, a, p], has_prev)
        copy = remote(kvb.at[1, j, a, p], kvb.at[2, j, a, p], fs.at[n, p], fr.at[j, a, p], device(1, core))
        start([copy], has_prev & has_next)

    def give_near(n, p):
        j, a = n // 2, half_of(n)
        copy = remote(ret1.at[n, p], rb1.at[2 * core + j, p], rs1.at[n, p], rr1.at[2 * core + j, p], device(-1, a))
        start([copy], has_prev)

    def near_own(n):
        dk, dv = block(n // 2, 1, half_of(n), core)
        near[n, 0] = dk
        near[n, 1] = dv

    def near_other(n, first=False):
        dk, dv = block(n // 2, 1, half_of(n), other, first)
        near[n, 0] += dk
        near[n, 1] += dv

    def far_block(n):
        j, a = n // 2, half_of(n)
        for p in range(2):
            arrived(kvb.at[2, j, a, p], fr.at[j, a, p], has_prev2)
        dk, dv = block(j, 2, a, 0)
        far[0] = dk
        far[1] = dv

        @pl.when(a == 1)
        def _():
            dk2, dv2 = block(j, 2, a, 1)
            far[0] += dk2
            far[1] += dv2

        for p in range(2):
            ret2[n, p] = far[p].astype(BF16)
            if n == 0:
                copy = remote(ret2.at[0, p], rb2.at[p], rs2.at[0, p], rr2.at[p], device(-2, a))
            else:
                copy = remote(ret2.at[n, p], pre.at[n, p], rs2.at[n, p], rp.at[n, p], device(-1, core))
            start([copy], has_prev2)

    def pass_on(n, p):
        arrived(pre.at[n, p], rp.at[n, p], has_prev & has_next)
        ret1[n, p] = (near[n, p] + pre[n, p].astype(F32)).astype(BF16)
        give_near(n, p)

    def give_queries(j):
        theirs = dq_acc[j][pl.ds(pl.multiple_of(other * rows, rows), rows), :] * scale
        dq_send[j] = theirs.astype(BF16).reshape(width, group, 128)
        remote(dq_send.at[j], dq_out.at[:, 2 * core + j], dqs.at[j], dqr.at[j], sibling).start()
        mine = dq_acc[j][pl.ds(pl.multiple_of(core * rows, rows), rows), :] * scale
        dq_out[:, 2 * core + j] = mine.astype(BF16).reshape(width, group, 128)

    swap_wait(0)
    row_terms(0, other)
    sibling_keys(0, True)
    forward(0, 0)
    late_rows(0)
    for query_half, key_half in ((0, 0), (0, 1), (1, 1)):
        mask(2, query_half, key_half)
    forward(0, 1)
    start(own(3), has_next)
    near_own(0)
    forward(1, 0)
    near_other(0)
    for p in range(2):
        ret1[0, p] = near[0, p].astype(BF16)
        give_near(0, p)
    forward(1, 1)
    swap_wait(1)
    near_own(1)
    row_terms(1, other)
    near_other(1)
    forward(2, 0)
    forward(2, 1)
    sibling_keys(1, True)
    near_own(2)
    near_other(2)
    far_block(0)
    forward(3, 0)
    late_rows(1)
    forward(3, 1)
    near_own(3)
    near_other(3)
    far_block(1)
    give_queries(0)
    far_block(2)
    far_block(3)
    give_queries(1)
    for n in range(1, 4):
        for p in range(2):
            pass_on(n, p)

    for n in range(4):
        j = n // 2
        h = 2 * half_of(n) + j
        if n % 2 == 1:
            arrived(rb0.at[j], rr0.at[j])
        for p in range(2):
            arrived(rb1.at[h, p], rr1.at[h, p], has_next)
            acc = rb1[h, p].astype(F32) + (parts[0, j, p] if n % 2 == 0 else rb0[j, p].astype(F32))
            if n == 0:
                arrived(rb2.at[p], rr2.at[p], has_next2)
                acc = acc + rb2[p].astype(F32)
            total[p, h] = acc.T
    dk_out[...] = jnp.transpose(total[0], (1, 0, 2)).astype(BF16)
    dv_out[...] = jnp.transpose(total[1], (1, 0, 2)).astype(BF16)

    for j in range(2):
        arrived(dq_out.at[:, 2 * other + j], dqr.at[j])
        sent(dq_send.at[j], dqs.at[j])
        sent(ret0.at[j], rs0.at[j])
    for copy in swaps:
        copy.wait_send()
    for n in range(4):
        for p in range(2):
            sent(own_kv.at[0, p], ks.at[n, p], has_next)
            sent(kvb.at[1, 0, 0, p], fs.at[n, p], has_prev & has_next)
            sent(ret1.at[n, p], rs1.at[n, p], has_prev)
            sent(ret2.at[n, p], rs2.at[n, p], has_prev2)


def hand_over(*refs):
    sems = refs[6]
    copies = [pltpu.make_async_copy(refs[i], refs[3 + i], sems.at[i]) for i in range(3)]
    for copy in copies:
        copy.start()
    for copy in copies:
        copy.wait()


def on_device(n_chips, queries, keys, values, attn_out, out_grad, log_sums, doc_ids):
    width, heads, size = queries.shape
    kv = keys.shape[1]
    group = heads // kv
    rows = width * group
    split = (width, kv, group, size)
    any_spec = pl.BlockSpec(memory_space=pl.ANY)
    vmem_spec = pl.BlockSpec(memory_space=pltpu.VMEM)
    dma = pltpu.SemaphoreType.DMA
    dq, dk, dv = pl.pallas_call(
        functools.partial(kernel, n_chips, width, group, size ** -0.5),
        out_shape=(
            pltpu.VMEM(split, BF16),
            pltpu.VMEM(keys.shape, BF16),
            pltpu.VMEM(keys.shape, BF16),
        ),
        in_specs=[any_spec] * 7,
        out_specs=(vmem_spec,) * 3,
        scratch_shapes=[
            pltpu.VMEM((2, 2, width, group, size), BF16),
            pltpu.VMEM((2, 2, width, group, size), BF16),
            pltpu.VMEM((2, 2, width, group, size), BF16),
            pltpu.VMEM((2, 2, group, width), F32),
            pltpu.VMEM((2 * n_chips, width), jnp.int32),
            pltpu.VMEM(keys.shape, BF16),
            pltpu.VMEM(keys.shape, BF16),
            pltpu.VMEM((kv, 2, width, size), BF16),
            pltpu.VMEM((3, 2, 2, 2, width, size), BF16),
            *[pltpu.VMEM((2, 2 * rows, width), F32)] * 3,
            *[pltpu.VMEM((2 * rows, 128), F32)] * 6,
            pltpu.VMEM((2, width, group, size), BF16),
            pltpu.VMEM((2, 2, 2, size, width), F32),
            pltpu.VMEM((4, 2, size, width), F32),
            pltpu.VMEM((2, size, width), F32),
            pltpu.VMEM((2, 2, size, width), BF16),
            pltpu.VMEM((4, 2, size, width), BF16),
            pltpu.VMEM((4, 2, size, width), BF16),
            pltpu.VMEM((2, 2, size, width), BF16),
            pltpu.VMEM((kv, 2, size, width), BF16),
            pltpu.VMEM((2, size, width), BF16),
            pltpu.VMEM((4, 2, size, width), BF16),
            pltpu.VMEM((2, kv, width, size), F32),
            dma((10,)), dma((7,)), dma((7,)), dma((4, 2)), dma((2,)), dma((2,)), dma((2, 2, 2)), dma((4, 2)),
            dma((2, 2, 2)), dma((2,)), dma((4, 2)), dma((4, 2)), dma((2,)), dma((kv, 2)), dma((2,)), dma((4, 2)),
            dma((2,)), dma((2,)),
        ],
        compiler_params=pltpu.CompilerParams(
            collective_id=0, has_side_effects=True, vmem_limit_bytes=56 * 2**20
        ),
    )(
        queries.reshape(split), keys, values, attn_out.reshape(split), out_grad.reshape(split),
        log_sums.reshape(kv, group, width), doc_ids.reshape(2 * n_chips, width),
    )
    dq, dk, dv = pl.pallas_call(
        hand_over,
        out_shape=tuple(jax.ShapeDtypeStruct(x.shape, x.dtype) for x in (dq, dk, dv)),
        in_specs=[vmem_spec] * 3,
        out_specs=(any_spec,) * 3,
        scratch_shapes=[dma((3,))],
        compiler_params=pltpu.CompilerParams(vmem_limit_bytes=2**20),
    )(dq, dk, dv)
    return dq.reshape(queries.shape), dk, dv


def solution(mesh):
    placed = (
        P(("dp", "seq"), None, None),
        P(("dp", "seq"), None, None),
        P(("dp", "seq"), None, None),
        P(("dp", "seq"), None, None),
        P(("dp", "seq"), None, None),
        P(None, ("dp", "seq")),
        P("dp"),
    )
    return jax.shard_map(
        functools.partial(on_device, mesh.shape["seq"] // 2),
        mesh=mesh,
        in_specs=placed,
        out_specs=(P(("dp", "seq"), None, None),) * 3,
        check_vma=False,
    )
```

```python
import functools

import jax
import jax.numpy as jnp
from jax import lax
from jax.experimental import pallas as pl
from jax.experimental.pallas import tpu as pltpu
from jax.sharding import PartitionSpec as P

F32 = jnp.float32
BF16 = jnp.bfloat16
MESH = pl.DeviceIdType.MESH
NT = (((1,), (1,)), ((), ()))
NN = (((1,), (0,)), ((), ()))
TN = (((0,), (0,)), ((), ()))
DIRECT = (0,)
LOG2E = 1.4426950408889634


def dot(a, b, dims):
    return lax.dot_general(a, b, dims, preferred_element_type=F32)


def kernel(n_chips, width, group, scale,
           q_hbm, k_hbm, v_hbm, o_hbm, g_hbm, lse_hbm, doc_hbm,
           dq_out, dk_out, dv_out,
           qs, gs, os_, lse_in, docs, kin, vin, own_kv, kvb, bias0, bias1, bias2, lse_b0, lse_b1, dl_b0, dl_b1, dq_acc0, dq_acc1, dq_send,
           parts, near, probs, ret0, ret1, ret2, rb0, rb1, rb2, pre, total,
           loc_sem, xs, xr, ks, ks0, kr0, kr1, fs, fr, rs0, rs1, rs2, rr0, rr1, rr2, rp, dqs, dqr):
    lse_b, dl_b, dq_acc = (lse_b0, lse_b1), (dl_b0, dl_b1), (dq_acc0, dq_acc1)
    bias = (bias0, bias1, bias2)
    me = lax.axis_index("seq")
    core = lax.rem(me, 2)
    chip = me // 2
    other = 1 - core
    rows = width * group

    def device(step, which):
        return {"seq": lax.rem(chip + step + n_chips, n_chips) * 2 + which}

    sibling = device(0, other)
    has_prev, has_next = chip > 0, chip < n_chips - 1
    has_prev2, has_next2 = chip > 1, chip < n_chips - 2

    barrier = pltpu.get_barrier_semaphore()

    @pl.when(has_prev)
    def _():
        pl.semaphore_signal(barrier, inc=1, device_id=device(-1, 0), device_id_type=MESH)
        pl.semaphore_signal(barrier, inc=1, device_id=device(-1, 1), device_id_type=MESH)

    pl.semaphore_signal(barrier, inc=1, device_id=sibling, device_id_type=MESH)

    def remote(src, dst, send, recv, to):
        return pltpu.make_async_remote_copy(
            src_ref=src, dst_ref=dst, send_sem=send, recv_sem=recv, device_id=to, device_id_type=MESH
        )

    def arrived(dst, sem, there=None):
        def wait():
            remote(dst, dst, xs.at[0], sem, sibling).wait_recv()

        wait() if there is None else pl.when(there)(wait)

    def sent(src, sem, there=None):
        def wait():
            remote(src, src, sem, xr.at[0], sibling).wait_send()

        wait() if there is None else pl.when(there)(wait)

    def start(copies, there):
        @pl.when(there)
        def _():
            for copy in copies:
                copy.start()

    @pl.when(chip == 0)
    def _():
        kvb[1] = jnp.zeros_like(kvb[1])

    @pl.when(jnp.logical_not(has_prev2))
    def _():
        kvb[2] = jnp.zeros_like(kvb[2])

    @pl.when(jnp.logical_not(has_next))
    def _():
        rb1[...] = jnp.zeros_like(rb1)

    @pl.when(jnp.logical_not(has_next & has_prev))
    def _():
        pre[...] = jnp.zeros_like(pre)

    @pl.when(jnp.logical_not(has_next2))
    def _():
        rb2[...] = jnp.zeros_like(rb2)

    local = [
        pltpu.make_async_copy(k_hbm, kin, loc_sem.at[0]),
        pltpu.make_async_copy(v_hbm, vin, loc_sem.at[1]),
        pltpu.make_async_copy(doc_hbm, docs, loc_sem.at[2]),
        pltpu.make_async_copy(lse_hbm.at[pl.ds(2 * core, 2)], lse_in.at[:, core], loc_sem.at[3]),
    ]
    for j in range(2):
        for i, (src, dst) in enumerate(((q_hbm, qs), (g_hbm, gs), (o_hbm, os_))):
            local.append(
                pltpu.make_async_copy(src.at[:, 2 * core + j], dst.at[j, core], loc_sem.at[4 + 3 * j + i])
            )
    for copy in local:
        copy.start()

    local[0].wait()
    own_kv[:, 0] = jnp.transpose(kin[...], (1, 0, 2))
    local[1].wait()
    own_kv[:, 1] = jnp.transpose(vin[...], (1, 0, 2))

    pl.semaphore_wait(barrier, jnp.where(has_next, 3, 1))

    def half_of(n):
        return (core, other)[n % 2]

    def own(n):
        j, which = n // 2, half_of(n)
        return [
            remote(own_kv.at[2 * which + j, p], kvb.at[1, j, core, p], ks.at[n, p], kr1.at[j, core, p], device(1, which))
            for p in range(2)
        ]

    start(own(0) + own(1) + own(2), has_next)
    swaps = [remote(lse_hbm.at[pl.ds(2 * other, 2)], lse_in.at[:, core], xs.at[6], xr.at[6], sibling)]
    for j in range(2):
        for i, (src, dst) in enumerate(((g_hbm, gs), (o_hbm, os_), (q_hbm, qs))):
            swaps.append(remote(src.at[:, 2 * other + j], dst.at[j, core], xs.at[3 * j + i], xr.at[3 * j + i], sibling))
        swaps.append(remote(own_kv.at[2 * other + j], kvb.at[0, j, core], ks0.at[j], kr0.at[j], sibling))
    for copy in swaps:
        copy.start()

    for j in range(2):
        kvb[0, j, core] = own_kv[2 * core + j]

    local[2].wait()

    def mask(back, query_half, key_half):
        key_chip = chip - back
        key_row = lax.rem(key_chip + n_chips, n_chips) * 2 + key_half
        query_row = chip * 2 + query_half
        key_doc = docs[pl.ds(key_row, 1), :].astype(F32)
        query_doc = docs[pl.ds(query_row, 1), :].astype(F32)
        query_col = jnp.broadcast_to(query_doc, (width, width)).T
        t = lax.broadcasted_iota(jnp.int32, (width, width), 0) + query_row * width
        p = lax.broadcasted_iota(jnp.int32, (width, width), 1) + (key_chip * 2 + key_half) * width
        live = (query_col == key_doc) & (p <= t) & (p >= 0)
        value = jnp.where(live, 0.0, -jnp.inf).astype(F32)
        wide = jnp.broadcast_to(value[:, None, :], (width, group, width)).reshape(rows, width)
        bias[back][key_half, query_half * rows:(query_half + 1) * rows, :] = wide

    for query_half, key_half in ((0, 0), (1, 0), (1, 1)):
        mask(0, query_half, key_half)

    def row_terms(j, half):
        start = pl.multiple_of(half * rows, rows)
        row = lse_in[j, half] * LOG2E
        lse_b[j][pl.ds(start, rows), :] = jnp.broadcast_to(row.T[:, :, None], (width, group, 128)).reshape(rows, 128)
        g = gs[j, half].reshape(rows, 128).astype(F32)
        o = os_[j, half].reshape(rows, 128).astype(F32)
        dl_b[j][pl.ds(start, rows), :] = jnp.broadcast_to(jnp.sum(g * o, axis=-1, keepdims=True), (rows, 128))

    def block(j, back, key_half, half, first=False):
        r = pl.ds(pl.multiple_of(half * rows, rows), rows)
        q = qs[j, half].reshape(rows, 128)
        g = gs[j, half].reshape(rows, 128)
        k = kvb[back, j, key_half, 0]
        v = kvb[back, j, key_half, 1]
        s = dot(q, k, NT)
        dp = dot(g, v, NT)
        p = jnp.exp2(s * (scale * LOG2E) - lse_b[j][r, :] + bias[back][key_half, r, :])
        ds = (p * (dp - dl_b[j][r, :])).astype(BF16)
        p = p.astype(BF16)
        term = dot(ds, k, NN)
        if first:
            dq_acc[j][r, :] = term
        else:
            dq_acc[j][r, :] += term
        return dot(q, ds, TN) * scale, dot(g, p, TN)

    for copy in local[3:]:
        copy.wait()

    for j in range(2):
        row_terms(j, core)
    for j in range(2):
        mask(1, j, 0)
        mask(1, j, 1)
        dk, dv = block(j, 0, core, core, True)
        parts[0, j, 0] = dk
        parts[0, j, 1] = dv

    arrived(lse_in.at[:, other], xr.at[6])

    def swap_wait(j):
        for i, dst in enumerate((gs, os_)):
            arrived(dst.at[j, other], xr.at[3 * j + i])

    def sibling_keys(j, first):
        arrived(qs.at[j, other], xr.at[3 * j + 2])
        arrived(kvb.at[0, j, other], kr0.at[j])
        dk, dv = block(j, 0, other, other, first)
        parts[1, j, 0] = dk
        parts[1, j, 1] = dv

    def late_rows(j):
        dk, dv = block(j, 0, 0, 1)
        parts[core, j, 0] += dk
        parts[core, j, 1] += dv
        ret0[j] = parts[1, j].astype(BF16)
        remote(ret0.at[j], rb0.at[j], rs0.at[j], rr0.at[j], sibling).start()

    def forward(n, p):
        j, a = n // 2, half_of(n)
        arrived(kvb.at[1, j, a, p], kr1.at[j, a, p], has_prev)
        copy = remote(kvb.at[1, j, a, p], kvb.at[2, j, a, p], fs.at[n, p], fr.at[j, a, p], device(1, core))
        start([copy], has_prev & has_next)

    def give_near(n, p):
        j, a = n // 2, half_of(n)
        copy = remote(ret1.at[n, p], rb1.at[2 * core + j, p], rs1.at[n, p], rr1.at[2 * core + j, p], device(-1, a))
        start([copy], has_prev)

    def near_own(n):
        dk, dv = block(n // 2, 1, half_of(n), core)
        near[n, 0] = dk
        near[n, 1] = dv

    def near_other(n, first=False):
        dk, dv = block(n // 2, 1, half_of(n), other, first)
        near[n, 0] += dk
        near[n, 1] += dv

    def near_done(n):
        if n in DIRECT:
            for p in range(2):
                ret1[n, p] = near[n, p].astype(BF16)
                give_near(n, p)

    def far_probs(j, key_half, half):
        r = pl.ds(half * rows, rows)
        g = gs[j, half].reshape(rows, 128)
        s = dot(qs[j, half].reshape(rows, 128), kvb[2, j, key_half, 0], NT)
        p = jnp.exp2(s * (scale * LOG2E) - lse_b[j][r, :] + bias[2][key_half, r, :])
        probs[r, :] = p
        return dot(g, p.astype(BF16), TN)

    def far_scores(j, key_half, half):
        r = pl.ds(half * rows, rows)
        dp = dot(gs[j, half].reshape(rows, 128), kvb[2, j, key_half, 1], NT)
        ds = (probs[r, :] * (dp - dl_b[j][r, :])).astype(BF16)
        dq_acc[j][r, :] += dot(ds, kvb[2, j, key_half, 0], NN)
        return dot(qs[j, half].reshape(rows, 128), ds, TN) * scale

    def far_block(n):
        j, a = n // 2, half_of(n)
        for p, part in ((1, far_probs), (0, far_scores)):
            arrived(kvb.at[2, j, a, 1 - p], fr.at[j, a, 1 - p], has_prev2)

            @pl.when(a == 0)
            def _():
                ret2[n, p] = part(j, a, 0).astype(BF16)

            @pl.when(a == 1)
            def _():
                ret2[n, p] = (part(j, a, 0) + part(j, a, 1)).astype(BF16)

            if n in DIRECT:
                copy = remote(ret2.at[n, p], rb2.at[n, p], rs2.at[n, p], rr2.at[n, p], device(-2, a))
            else:
                copy = remote(ret2.at[n, p], pre.at[n, p], rs2.at[n, p], rp.at[n, p], device(-1, core))
            start([copy], has_prev2)

    def pass_on(n, p):
        arrived(pre.at[n, p], rp.at[n, p], has_prev & has_next)
        ret1[n, p] = (near[n, p] + pre[n, p].astype(F32)).astype(BF16)
        give_near(n, p)

    def give_queries(j):
        theirs = dq_acc[j][pl.ds(pl.multiple_of(other * rows, rows), rows), :] * scale
        dq_send[j] = theirs.astype(BF16).reshape(width, group, 128)
        remote(dq_send.at[j], dq_out.at[:, 2 * core + j], dqs.at[j], dqr.at[j], sibling).start()
        mine = dq_acc[j][pl.ds(pl.multiple_of(core * rows, rows), rows), :] * scale
        dq_out[:, 2 * core + j] = mine.astype(BF16).reshape(width, group, 128)

    swap_wait(0)
    row_terms(0, other)
    sibling_keys(0, True)
    forward(0, 0)
    late_rows(0)
    for query_half, key_half in ((0, 0), (0, 1), (1, 1)):
        mask(2, query_half, key_half)
    forward(0, 1)
    start(own(3), has_next)
    near_own(0)
    forward(1, 0)
    near_other(0)
    near_done(0)
    forward(1, 1)
    swap_wait(1)
    near_own(1)
    row_terms(1, other)
    near_other(1)
    near_done(1)
    forward(2, 0)
    forward(2, 1)
    sibling_keys(1, True)
    near_own(2)
    near_other(2)
    near_done(2)
    far_block(0)
    forward(3, 0)
    late_rows(1)
    forward(3, 1)
    near_own(3)
    near_other(3)
    near_done(3)
    far_block(1)
    give_queries(0)
    far_block(2)
    far_block(3)
    give_queries(1)
    for n in range(4):
        for p in (1, 0):
            if n not in DIRECT:
                pass_on(n, p)

    for j in range(2):
        arrived(rb0.at[j], rr0.at[j])
        arrived(dq_out.at[:, 2 * other + j], dqr.at[j])
        sent(dq_send.at[j], dqs.at[j])
        sent(ret0.at[j], rs0.at[j])
    for copy in swaps:
        copy.wait_send()

    def finish(n, p):
        j = n // 2
        h = 2 * half_of(n) + j
        if True:
            arrived(rb1.at[h, p], rr1.at[h, p], has_next)
            acc = rb1[h, p].astype(F32) + (parts[0, j, p] if n % 2 == 0 else rb0[j, p].astype(F32))
            if n in DIRECT:
                arrived(rb2.at[n, p], rr2.at[n, p], has_next2)
                acc = acc + rb2[n, p].astype(F32)
            total[p, h] = acc.T

    for n in range(3):
        for p in (1, 0):
            finish(n, p)
    finish(3, 1)
    dv_out[...] = jnp.transpose(total[1], (1, 0, 2)).astype(BF16)
    for n in range(4):
        for p in range(2):
            sent(own_kv.at[0, p], ks.at[n, p], has_next)
            sent(kvb.at[1, 0, 0, p], fs.at[n, p], has_prev & has_next)
            sent(ret1.at[n, p], rs1.at[n, p], has_prev)
            sent(ret2.at[n, p], rs2.at[n, p], has_prev2)
    finish(3, 0)
    dk_out[...] = jnp.transpose(total[0], (1, 0, 2)).astype(BF16)


def hand_over(*refs):
    sems = refs[6]
    copies = [pltpu.make_async_copy(refs[i], refs[3 + i], sems.at[i]) for i in range(3)]
    for copy in copies:
        copy.start()
    for copy in copies:
        copy.wait()


def on_device(n_chips, queries, keys, values, attn_out, out_grad, log_sums, doc_ids):
    width, heads, size = queries.shape
    kv = keys.shape[1]
    group = heads // kv
    rows = width * group
    split = (width, kv, group, size)
    any_spec = pl.BlockSpec(memory_space=pl.ANY)
    vmem_spec = pl.BlockSpec(memory_space=pltpu.VMEM)
    dma = pltpu.SemaphoreType.DMA
    dq, dk, dv = pl.pallas_call(
        functools.partial(kernel, n_chips, width, group, size ** -0.5),
        out_shape=(
            pltpu.VMEM(split, BF16),
            pltpu.VMEM(keys.shape, BF16),
            pltpu.VMEM(keys.shape, BF16),
        ),
        in_specs=[any_spec] * 7,
        out_specs=(vmem_spec,) * 3,
        scratch_shapes=[
            pltpu.VMEM((2, 2, width, group, size), BF16),
            pltpu.VMEM((2, 2, width, group, size), BF16),
            pltpu.VMEM((2, 2, width, group, size), BF16),
            pltpu.VMEM((2, 2, group, width), F32),
            pltpu.VMEM((2 * n_chips, width), jnp.int32),
            pltpu.VMEM(keys.shape, BF16),
            pltpu.VMEM(keys.shape, BF16),
            pltpu.VMEM((kv, 2, width, size), BF16),
            pltpu.VMEM((3, 2, 2, 2, width, size), BF16),
            *[pltpu.VMEM((2, 2 * rows, width), F32)] * 3,
            *[pltpu.VMEM((2 * rows, 128), F32)] * 6,
            pltpu.VMEM((2, width, group, size), BF16),
            pltpu.VMEM((2, 2, 2, size, width), F32),
            pltpu.VMEM((4, 2, size, width), F32),
            pltpu.VMEM((2 * rows, width), F32),
            pltpu.VMEM((2, 2, size, width), BF16),
            pltpu.VMEM((4, 2, size, width), BF16),
            pltpu.VMEM((4, 2, size, width), BF16),
            pltpu.VMEM((2, 2, size, width), BF16),
            pltpu.VMEM((kv, 2, size, width), BF16),
            pltpu.VMEM((4, 2, size, width), BF16),
            pltpu.VMEM((4, 2, size, width), BF16),
            pltpu.VMEM((2, kv, width, size), F32),
            dma((10,)), dma((7,)), dma((7,)), dma((4, 2)), dma((2,)), dma((2,)), dma((2, 2, 2)), dma((4, 2)),
            dma((2, 2, 2)), dma((2,)), dma((4, 2)), dma((4, 2)), dma((2,)), dma((kv, 2)), dma((4, 2)), dma((4, 2)),
            dma((2,)), dma((2,)),
        ],
        compiler_params=pltpu.CompilerParams(
            collective_id=0, has_side_effects=True, vmem_limit_bytes=56 * 2**20
        ),
    )(
        queries.reshape(split), keys, values, attn_out.reshape(split), out_grad.reshape(split),
        log_sums.reshape(kv, group, width), doc_ids.reshape(2 * n_chips, width),
    )
    dq, dk, dv = pl.pallas_call(
        hand_over,
        out_shape=tuple(jax.ShapeDtypeStruct(x.shape, x.dtype) for x in (dq, dk, dv)),
        in_specs=[vmem_spec] * 3,
        out_specs=(any_spec,) * 3,
        scratch_shapes=[dma((3,))],
        compiler_params=pltpu.CompilerParams(vmem_limit_bytes=2**20),
    )(dq, dk, dv)
    return dq.reshape(queries.shape), dk, dv


def solution(mesh):
    placed = (
        P(("dp", "seq"), None, None),
        P(("dp", "seq"), None, None),
        P(("dp", "seq"), None, None),
        P(("dp", "seq"), None, None),
        P(("dp", "seq"), None, None),
        P(None, ("dp", "seq")),
        P("dp"),
    )
    return jax.shard_map(
        functools.partial(on_device, mesh.shape["seq"] // 2),
        mesh=mesh,
        in_specs=placed,
        out_specs=(P(("dp", "seq"), None, None),) * 3,
        check_vma=False,
    )
```

```python
import functools

import jax
import jax.numpy as jnp
from jax import lax
from jax.experimental import pallas as pl
from jax.experimental.pallas import tpu as pltpu
from jax.sharding import PartitionSpec as P

F32 = jnp.float32
BF16 = jnp.bfloat16
MESH = pl.DeviceIdType.MESH
NT = (((1,), (1,)), ((), ()))
NN = (((1,), (0,)), ((), ()))
TN = (((0,), (0,)), ((), ()))
DIRECT = ((0, 0), (0, 1), (1, 1))
LOG2E = 1.4426950408889634


def dot(a, b, dims):
    return lax.dot_general(a, b, dims, preferred_element_type=F32)


def kernel(n_chips, width, group, scale,
           q_hbm, k_hbm, v_hbm, o_hbm, g_hbm, lse_hbm, doc_hbm,
           dq_out, dk_out, dv_out,
           qs, gs, os_, lse_in, docs, kin, vin, own_kv, kvb, bias0, bias1, bias2, lse_b0, lse_b1, dl_b0, dl_b1, dq_acc0, dq_acc1, dq_send,
           parts, near, probs, ret0, ret1, ret2, rb0, rb1, rb2, pre, total,
           loc_sem, xs, xr, ks, ks0, kr0, kr1, fs, fr, rs0, rs1, rs2, rr0, rr1, rr2, rp, dqs, dqr):
    lse_b, dl_b, dq_acc = (lse_b0, lse_b1), (dl_b0, dl_b1), (dq_acc0, dq_acc1)
    bias = (bias0, bias1, bias2)
    me = lax.axis_index("seq")
    core = lax.rem(me, 2)
    chip = me // 2
    other = 1 - core
    rows = width * group

    def device(step, which):
        return {"seq": lax.rem(chip + step + n_chips, n_chips) * 2 + which}

    sibling = device(0, other)
    has_prev, has_next = chip > 0, chip < n_chips - 1
    has_prev2, has_next2 = chip > 1, chip < n_chips - 2

    barrier = pltpu.get_barrier_semaphore()

    @pl.when(has_prev)
    def _():
        pl.semaphore_signal(barrier, inc=1, device_id=device(-1, 0), device_id_type=MESH)
        pl.semaphore_signal(barrier, inc=1, device_id=device(-1, 1), device_id_type=MESH)

    pl.semaphore_signal(barrier, inc=1, device_id=sibling, device_id_type=MESH)

    def remote(src, dst, send, recv, to):
        return pltpu.make_async_remote_copy(
            src_ref=src, dst_ref=dst, send_sem=send, recv_sem=recv, device_id=to, device_id_type=MESH
        )

    def arrived(dst, sem, there=None):
        def wait():
            remote(dst, dst, xs.at[0], sem, sibling).wait_recv()

        wait() if there is None else pl.when(there)(wait)

    def sent(src, sem, there=None):
        def wait():
            remote(src, src, sem, xr.at[0], sibling).wait_send()

        wait() if there is None else pl.when(there)(wait)

    def start(copies, there):
        @pl.when(there)
        def _():
            for copy in copies:
                copy.start()

    @pl.when(chip == 0)
    def _():
        kvb[1] = jnp.zeros_like(kvb[1])

    @pl.when(jnp.logical_not(has_prev2))
    def _():
        kvb[2] = jnp.zeros_like(kvb[2])

    @pl.when(jnp.logical_not(has_next))
    def _():
        rb1[...] = jnp.zeros_like(rb1)

    @pl.when(jnp.logical_not(has_next & has_prev))
    def _():
        pre[...] = jnp.zeros_like(pre)

    @pl.when(jnp.logical_not(has_next2))
    def _():
        rb2[...] = jnp.zeros_like(rb2)

    local = [
        pltpu.make_async_copy(k_hbm, kin, loc_sem.at[0]),
        pltpu.make_async_copy(v_hbm, vin, loc_sem.at[1]),
        pltpu.make_async_copy(doc_hbm, docs, loc_sem.at[2]),
        pltpu.make_async_copy(lse_hbm.at[pl.ds(2 * core, 2)], lse_in.at[:, core], loc_sem.at[3]),
    ]
    for j in range(2):
        for i, (src, dst) in enumerate(((q_hbm, qs), (g_hbm, gs), (o_hbm, os_))):
            local.append(
                pltpu.make_async_copy(src.at[:, 2 * core + j], dst.at[j, core], loc_sem.at[4 + 3 * j + i])
            )
    for copy in local:
        copy.start()

    local[0].wait()
    own_kv[:, 0] = jnp.transpose(kin[...], (1, 0, 2))
    local[1].wait()
    own_kv[:, 1] = jnp.transpose(vin[...], (1, 0, 2))

    pl.semaphore_wait(barrier, jnp.where(has_next, 3, 1))

    def half_of(n):
        return (core, other)[n % 2]

    def own(n):
        j, which = n // 2, half_of(n)
        return [
            remote(own_kv.at[2 * which + j, p], kvb.at[1, j, core, p], ks.at[n, p], kr1.at[j, core, p], device(1, which))
            for p in range(2)
        ]

    start(own(0) + own(1) + own(2), has_next)
    swaps = [remote(lse_hbm.at[pl.ds(2 * other, 2)], lse_in.at[:, core], xs.at[6], xr.at[6], sibling)]
    for j in range(2):
        for i, (src, dst) in enumerate(((g_hbm, gs), (o_hbm, os_), (q_hbm, qs))):
            swaps.append(remote(src.at[:, 2 * other + j], dst.at[j, core], xs.at[3 * j + i], xr.at[3 * j + i], sibling))
        swaps.append(remote(own_kv.at[2 * other + j], kvb.at[0, j, core], ks0.at[j], kr0.at[j], sibling))
    for copy in swaps:
        copy.start()

    for j in range(2):
        kvb[0, j, core] = own_kv[2 * core + j]

    local[2].wait()

    def mask(back, query_half, key_half):
        key_chip = chip - back
        key_row = lax.rem(key_chip + n_chips, n_chips) * 2 + key_half
        query_row = chip * 2 + query_half
        key_doc = docs[pl.ds(key_row, 1), :].astype(F32)
        query_doc = docs[pl.ds(query_row, 1), :].astype(F32)
        query_col = jnp.broadcast_to(query_doc, (width, width)).T
        t = lax.broadcasted_iota(jnp.int32, (width, width), 0) + query_row * width
        p = lax.broadcasted_iota(jnp.int32, (width, width), 1) + (key_chip * 2 + key_half) * width
        live = (query_col == key_doc) & (p <= t) & (p >= 0)
        value = jnp.where(live, 0.0, -jnp.inf).astype(F32)
        wide = jnp.broadcast_to(value[:, None, :], (width, group, width)).reshape(rows, width)
        bias[back][key_half, query_half * rows:(query_half + 1) * rows, :] = wide

    for query_half, key_half in ((0, 0), (1, 0), (1, 1)):
        mask(0, query_half, key_half)

    def row_terms(j, half):
        start = pl.multiple_of(half * rows, rows)
        row = lse_in[j, half] * LOG2E
        lse_b[j][pl.ds(start, rows), :] = jnp.broadcast_to(row.T[:, :, None], (width, group, 128)).reshape(rows, 128)
        g = gs[j, half].reshape(rows, 128).astype(F32)
        o = os_[j, half].reshape(rows, 128).astype(F32)
        dl_b[j][pl.ds(start, rows), :] = jnp.broadcast_to(jnp.sum(g * o, axis=-1, keepdims=True), (rows, 128))

    def block(j, back, key_half, half, first=False):
        r = pl.ds(pl.multiple_of(half * rows, rows), rows)
        q = qs[j, half].reshape(rows, 128)
        g = gs[j, half].reshape(rows, 128)
        k = kvb[back, j, key_half, 0]
        v = kvb[back, j, key_half, 1]
        s = dot(q, k, NT)
        dp = dot(g, v, NT)
        p = jnp.exp2(s * (scale * LOG2E) - lse_b[j][r, :] + bias[back][key_half, r, :])
        ds = (p * (dp - dl_b[j][r, :])).astype(BF16)
        p = p.astype(BF16)
        term = dot(ds, k, NN)
        if first:
            dq_acc[j][r, :] = term
        else:
            dq_acc[j][r, :] += term
        return dot(q, ds, TN) * scale, dot(g, p, TN)

    for copy in local[3:]:
        copy.wait()

    for j in range(2):
        row_terms(j, core)
    for j in range(2):
        mask(1, j, 0)
        mask(1, j, 1)
        dk, dv = block(j, 0, core, core, True)
        parts[0, j, 0] = dk
        parts[0, j, 1] = dv

    arrived(lse_in.at[:, other], xr.at[6])

    def swap_wait(j):
        for i, dst in enumerate((gs, os_)):
            arrived(dst.at[j, other], xr.at[3 * j + i])

    def sibling_keys(j, first):
        arrived(qs.at[j, other], xr.at[3 * j + 2])
        arrived(kvb.at[0, j, other], kr0.at[j])
        dk, dv = block(j, 0, other, other, first)
        parts[1, j, 0] = dk
        parts[1, j, 1] = dv

    def late_rows(j):
        dk, dv = block(j, 0, 0, 1)
        parts[core, j, 0] += dk
        parts[core, j, 1] += dv
        ret0[j] = parts[1, j].astype(BF16)
        remote(ret0.at[j], rb0.at[j], rs0.at[j], rr0.at[j], sibling).start()

    def forward(n, p):
        j, a = n // 2, half_of(n)
        arrived(kvb.at[1, j, a, p], kr1.at[j, a, p], has_prev)
        copy = remote(kvb.at[1, j, a, p], kvb.at[2, j, a, p], fs.at[n, p], fr.at[j, a, p], device(1, core))
        start([copy], has_prev & has_next)

    def give_near(n, p):
        j, a = n // 2, half_of(n)
        copy = remote(ret1.at[n, p], rb1.at[2 * core + j, p], rs1.at[n, p], rr1.at[2 * core + j, p], device(-1, a))
        start([copy], has_prev)

    def near_own(n):
        dk, dv = block(n // 2, 1, half_of(n), core)
        near[n, 0] = dk
        near[n, 1] = dv

    def near_other(n, first=False):
        dk, dv = block(n // 2, 1, half_of(n), other, first)
        near[n, 0] += dk
        near[n, 1] += dv

    def near_done(n):
        for p in range(2):
            if (n, p) in DIRECT:
                ret1[n, p] = near[n, p].astype(BF16)
                give_near(n, p)

    def far_probs(j, key_half, half):
        r = pl.ds(half * rows, rows)
        g = gs[j, half].reshape(rows, 128)
        s = dot(qs[j, half].reshape(rows, 128), kvb[2, j, key_half, 0], NT)
        p = jnp.exp2(s * (scale * LOG2E) - lse_b[j][r, :] + bias[2][key_half, r, :])
        probs[r, :] = p
        return dot(g, p.astype(BF16), TN)

    def far_scores(j, key_half, half):
        r = pl.ds(half * rows, rows)
        dp = dot(gs[j, half].reshape(rows, 128), kvb[2, j, key_half, 1], NT)
        ds = (probs[r, :] * (dp - dl_b[j][r, :])).astype(BF16)
        dq_acc[j][r, :] += dot(ds, kvb[2, j, key_half, 0], NN)
        return dot(qs[j, half].reshape(rows, 128), ds, TN) * scale

    def far_block(n):
        j, a = n // 2, half_of(n)
        for p, part in ((1, far_probs), (0, far_scores)):
            arrived(kvb.at[2, j, a, 1 - p], fr.at[j, a, 1 - p], has_prev2)

            @pl.when(a == 0)
            def _():
                ret2[n, p] = part(j, a, 0).astype(BF16)

            @pl.when(a == 1)
            def _():
                ret2[n, p] = (part(j, a, 0) + part(j, a, 1)).astype(BF16)

            if (n, p) in DIRECT:
                copy = remote(ret2.at[n, p], rb2.at[n, p], rs2.at[n, p], rr2.at[n, p], device(-2, a))
            else:
                copy = remote(ret2.at[n, p], pre.at[n, p], rs2.at[n, p], rp.at[n, p], device(-1, core))
            start([copy], has_prev2)

    def pass_on(n, p):
        arrived(pre.at[n, p], rp.at[n, p], has_prev & has_next)
        ret1[n, p] = (near[n, p] + pre[n, p].astype(F32)).astype(BF16)
        give_near(n, p)

    def give_queries(j):
        theirs = dq_acc[j][pl.ds(pl.multiple_of(other * rows, rows), rows), :] * scale
        dq_send[j] = theirs.astype(BF16).reshape(width, group, 128)
        remote(dq_send.at[j], dq_out.at[:, 2 * core + j], dqs.at[j], dqr.at[j], sibling).start()
        mine = dq_acc[j][pl.ds(pl.multiple_of(core * rows, rows), rows), :] * scale
        dq_out[:, 2 * core + j] = mine.astype(BF16).reshape(width, group, 128)

    swap_wait(0)
    row_terms(0, other)
    sibling_keys(0, True)
    forward(0, 0)
    late_rows(0)
    for query_half, key_half in ((0, 0), (0, 1), (1, 1)):
        mask(2, query_half, key_half)
    forward(0, 1)
    start(own(3), has_next)
    near_own(0)
    forward(1, 0)
    near_other(0)
    near_done(0)
    forward(1, 1)
    swap_wait(1)
    near_own(1)
    row_terms(1, other)
    near_other(1)
    near_done(1)
    forward(2, 0)
    forward(2, 1)
    sibling_keys(1, True)
    near_own(2)
    near_other(2)
    near_done(2)
    far_block(0)
    forward(3, 0)
    late_rows(1)
    forward(3, 1)
    near_own(3)
    near_other(3)
    near_done(3)
    far_block(1)
    give_queries(0)
    far_block(2)
    far_block(3)
    give_queries(1)
    for n in range(4):
        for p in (1, 0):
            if (n, p) not in DIRECT:
                pass_on(n, p)

    for j in range(2):
        arrived(rb0.at[j], rr0.at[j])
        arrived(dq_out.at[:, 2 * other + j], dqr.at[j])
        sent(dq_send.at[j], dqs.at[j])
        sent(ret0.at[j], rs0.at[j])
    for copy in swaps:
        copy.wait_send()

    def finish(n, p):
        j = n // 2
        h = 2 * half_of(n) + j
        if True:
            arrived(rb1.at[h, p], rr1.at[h, p], has_next)
            acc = rb1[h, p].astype(F32) + (parts[0, j, p] if n % 2 == 0 else rb0[j, p].astype(F32))
            if (n, p) in DIRECT:
                arrived(rb2.at[n, p], rr2.at[n, p], has_next2)
                acc = acc + rb2[n, p].astype(F32)
            total[p, h] = acc.T

    for n in range(3):
        for p in (1, 0):
            finish(n, p)
    finish(3, 1)
    dv_out[...] = jnp.transpose(total[1], (1, 0, 2)).astype(BF16)
    for n in range(4):
        for p in range(2):
            sent(own_kv.at[0, p], ks.at[n, p], has_next)
            sent(kvb.at[1, 0, 0, p], fs.at[n, p], has_prev & has_next)
            sent(ret1.at[n, p], rs1.at[n, p], has_prev)
            sent(ret2.at[n, p], rs2.at[n, p], has_prev2)
    finish(3, 0)
    dk_out[...] = jnp.transpose(total[0], (1, 0, 2)).astype(BF16)


def hand_over(*refs):
    sems = refs[6]
    copies = [pltpu.make_async_copy(refs[i], refs[3 + i], sems.at[i]) for i in range(3)]
    for copy in copies:
        copy.start()
    for copy in copies:
        copy.wait()


def on_device(n_chips, queries, keys, values, attn_out, out_grad, log_sums, doc_ids):
    width, heads, size = queries.shape
    kv = keys.shape[1]
    group = heads // kv
    rows = width * group
    split = (width, kv, group, size)
    any_spec = pl.BlockSpec(memory_space=pl.ANY)
    vmem_spec = pl.BlockSpec(memory_space=pltpu.VMEM)
    dma = pltpu.SemaphoreType.DMA
    dq, dk, dv = pl.pallas_call(
        functools.partial(kernel, n_chips, width, group, size ** -0.5),
        out_shape=(
            pltpu.VMEM(split, BF16),
            pltpu.VMEM(keys.shape, BF16),
            pltpu.VMEM(keys.shape, BF16),
        ),
        in_specs=[any_spec] * 7,
        out_specs=(vmem_spec,) * 3,
        scratch_shapes=[
            pltpu.VMEM((2, 2, width, group, size), BF16),
            pltpu.VMEM((2, 2, width, group, size), BF16),
            pltpu.VMEM((2, 2, width, group, size), BF16),
            pltpu.VMEM((2, 2, group, width), F32),
            pltpu.VMEM((2 * n_chips, width), jnp.int32),
            pltpu.VMEM(keys.shape, BF16),
            pltpu.VMEM(keys.shape, BF16),
            pltpu.VMEM((kv, 2, width, size), BF16),
            pltpu.VMEM((3, 2, 2, 2, width, size), BF16),
            *[pltpu.VMEM((2, 2 * rows, width), F32)] * 3,
            *[pltpu.VMEM((2 * rows, 128), F32)] * 6,
            pltpu.VMEM((2, width, group, size), BF16),
            pltpu.VMEM((2, 2, 2, size, width), F32),
            pltpu.VMEM((4, 2, size, width), F32),
            pltpu.VMEM((2 * rows, width), F32),
            pltpu.VMEM((2, 2, size, width), BF16),
            pltpu.VMEM((4, 2, size, width), BF16),
            pltpu.VMEM((4, 2, size, width), BF16),
            pltpu.VMEM((2, 2, size, width), BF16),
            pltpu.VMEM((kv, 2, size, width), BF16),
            pltpu.VMEM((4, 2, size, width), BF16),
            pltpu.VMEM((4, 2, size, width), BF16),
            pltpu.VMEM((2, kv, width, size), F32),
            dma((10,)), dma((7,)), dma((7,)), dma((4, 2)), dma((2,)), dma((2,)), dma((2, 2, 2)), dma((4, 2)),
            dma((2, 2, 2)), dma((2,)), dma((4, 2)), dma((4, 2)), dma((2,)), dma((kv, 2)), dma((4, 2)), dma((4, 2)),
            dma((2,)), dma((2,)),
        ],
        compiler_params=pltpu.CompilerParams(
            collective_id=0, has_side_effects=True, vmem_limit_bytes=56 * 2**20
        ),
    )(
        queries.reshape(split), keys, values, attn_out.reshape(split), out_grad.reshape(split),
        log_sums.reshape(kv, group, width), doc_ids.reshape(2 * n_chips, width),
    )
    dq, dk, dv = pl.pallas_call(
        hand_over,
        out_shape=tuple(jax.ShapeDtypeStruct(x.shape, x.dtype) for x in (dq, dk, dv)),
        in_specs=[vmem_spec] * 3,
        out_specs=(any_spec,) * 3,
        scratch_shapes=[dma((3,))],
        compiler_params=pltpu.CompilerParams(vmem_limit_bytes=2**20),
    )(dq, dk, dv)
    return dq.reshape(queries.shape), dk, dv


def solution(mesh):
    placed = (
        P(("dp", "seq"), None, None),
        P(("dp", "seq"), None, None),
        P(("dp", "seq"), None, None),
        P(("dp", "seq"), None, None),
        P(("dp", "seq"), None, None),
        P(None, ("dp", "seq")),
        P("dp"),
    )
    return jax.shard_map(
        functools.partial(on_device, mesh.shape["seq"] // 2),
        mesh=mesh,
        in_specs=placed,
        out_specs=(P(("dp", "seq"), None, None),) * 3,
        check_vma=False,
    )
```
